512 devices in a mesh: ctx: 64 (over y, z_lo, core), mp: 8 (over x, z_hi).
Axes of the slice: x: 4, y: 4, z: 16 (z_hi: 2, z_lo: 8; z = z_hi * 8 + z_lo), core: 2. Of those that a mesh axis runs over, the one named last changes fastest.
Arguments:
- stream: bfloat16 [4, 65536, 1024], P(None, 'ctx', 'mp'), may hold values from -40 to 40
- gain_mix: bfloat16 [1024], P('mp'), may hold values from 0.25 to 1.75
- proj_in: bfloat16 [8, 128, 384], P('mp'), may hold values from -0.5 to 0.5
- short_taps: float32 [3, 8, 384], P(None, 'mp'), may hold values from -3 to 3
- fwd_inner: bfloat16 [256, 256], replicated, may hold values from -0.375 to 0.375
- twid_inner: float32 [256, 256], P('ctx'), may hold values from -1.5 to 1.5
- fwd_outer: bfloat16 [256, 256], replicated, may hold values from -0.375 to 0.375
- kernel: bfloat16 [256, 256, 1024], P(None, 'ctx', 'mp'), may hold values from -4 to 4
- inv_outer: bfloat16 [256, 256], replicated, may hold values from -0.375 to 0.375
- backward_twiddle: float32 [256, 256], P(None, 'ctx'), may hold values from -1.5 to 1.5
- inv_inner: bfloat16 [256, 256], replicated, may hold values from -0.375 to 0.375
- proj_out: bfloat16 [8, 128, 128], P('mp'), may hold values from -0.5 to 0.5
- gain_mlp: bfloat16 [1024], P('mp'), may hold values from 0.25 to 1.75
- up_blocks: bfloat16 [8, 128, 512], P('mp'), may hold values from -0.5 to 0.5
- down_blocks: bfloat16 [8, 512, 128], P('mp'), may hold values from -0.25 to 0.25
Outputs:
- stream_out: bfloat16 [4, 65536, 1024], P(None, 'ctx', 'mp')
The draws below stay inside these ranges and needn't reach their ends.
All inputs are finite; a program needn't handle non-finite values.
Results may differ from the reference program's by a relative error of at most 0.0085.
Values may be sent and summed in bfloat16 or wider, within the bound.
A program may use at most 64 MiB of HBM per device.

```python
import jax
import jax.numpy as jnp
from jax import lax

D = 1024
FF = 4096
NB = 8
ROOT = 256
SEQS = 4
SEQ_LEN = 65536
CB = 128
HB = 512


def draw_stream(key, part):
    key_base, key_col, key_row = jax.random.split(key, 3)
    span = jnp.arange(D, dtype=jnp.float32) / D
    column_scale = jnp.exp(jnp.log(3.0) * span + jax.random.uniform(key_col, (D,), jnp.float32, 0.0, jnp.log(3.3))) / 3.0
    row_scale = jnp.exp(jax.random.uniform(key_row, (SEQS, SEQ_LEN, 1), jnp.float32, jnp.log(0.3), jnp.log(3.0)))
    base = jnp.clip(jax.random.normal(key_base, (SEQS, SEQ_LEN, D), jnp.float32), -4.0, 4.0)
    return (base * row_scale * column_scale).astype(jnp.bfloat16)


def levels(key, extent, cuts, smallest, top_value):
    def one(position, blocks):
        draws = jax.random.uniform(jax.random.fold_in(jax.random.fold_in(key, 6), position), (blocks,), jnp.float32, smallest / len(cuts), top_value / len(cuts))
        return jnp.repeat(jnp.exp(draws), extent[position] // blocks).reshape((-1,) + (1,) * (len(extent) - position - 1))

    gain = one(*cuts[0])
    for cut in cuts[1:]:
        gain = gain * one(*cut)
    return gain


def scatter_about(stream_key, extent, scale, most, shards=(), kind=jnp.bfloat16):
    values = jax.random.normal(stream_key, extent, jnp.float32) * scale
    if len(shards) > 0:
        values = levels(stream_key, extent, shards, -0.22, 0.18) * values
    return jnp.clip(values, min=-most, max=most).astype(kind)


def setup_inputs(seed: int = 0) -> dict:
    key_list = jax.random.split(jax.random.key(seed), 16)
    stream = draw_stream(jax.random.fold_in(key_list[15], 71), 0)
    gain_mix = jnp.clip(1.0 + 0.15 * jax.random.normal(key_list[1], (D,), jnp.float32), 0.25, 1.75).astype(jnp.bfloat16)
    proj_in = scatter_about(key_list[2], (NB, CB, 3 * CB), CB ** -0.5, 0.5, ((0, 8),))
    short_taps = scatter_about(key_list[3], (3, NB, 3 * CB), 0.5, 3.0, ((1, 8),), jnp.float32)
    fwd_inner = scatter_about(key_list[4], (ROOT, ROOT), ROOT ** -0.5, 0.375)
    twid_inner = jnp.clip(jax.random.uniform(key_list[5], (ROOT, ROOT), jnp.float32, -1.5, 1.5) * levels(key_list[5], (ROOT, ROOT), ((0, 64),), -0.4, 0.0), -1.5, 1.5)
    fwd_outer = scatter_about(key_list[6], (ROOT, ROOT), ROOT ** -0.5, 0.375)
    kernel = scatter_about(key_list[7], (ROOT, ROOT, D), 1.0, 4.0, ((1, 64), (2, 8)))
    inv_outer = scatter_about(key_list[8], (ROOT, ROOT), ROOT ** -0.5, 0.375)
    backward_twiddle = jnp.clip(jax.random.uniform(key_list[9], (ROOT, ROOT), jnp.float32, -1.5, 1.5) * levels(key_list[9], (ROOT, ROOT), ((1, 64),), -0.4, 0.0), -1.5, 1.5)
    inv_inner = scatter_about(key_list[10], (ROOT, ROOT), ROOT ** -0.5, 0.375)
    proj_out = scatter_about(key_list[11], (NB, CB, CB), CB ** -0.5, 0.5, ((0, 8),))
    gain_mlp = jnp.clip(1.0 + 0.15 * jax.random.normal(key_list[12], (D,), jnp.float32), 0.25, 1.75).astype(jnp.bfloat16)
    up_blocks = scatter_about(key_list[13], (NB, CB, HB), CB ** -0.5, 0.5, ((0, 8),))
    down_blocks = scatter_about(key_list[14], (NB, HB, CB), HB ** -0.5, 0.25, ((0, 8),))
    return dict(stream=stream, gain_mix=gain_mix, proj_in=proj_in, short_taps=short_taps, fwd_inner=fwd_inner, twid_inner=twid_inner, fwd_outer=fwd_outer, kernel=kernel, inv_outer=inv_outer, backward_twiddle=backward_twiddle, inv_inner=inv_inner, proj_out=proj_out, gain_mlp=gain_mlp, up_blocks=up_blocks, down_blocks=down_blocks)


epsilon = 1e-05

def cast_bfloat16(value):
    return lax.optimization_barrier(value.astype(jnp.bfloat16))

def reference(stream, gain_mix, proj_in, short_taps, fwd_inner, twid_inner, fwd_outer, kernel, inv_outer, backward_twiddle, inv_inner, proj_out, gain_mlp, up_blocks, down_blocks):
    block_width = D // NB
    sub_width = block_width // NB
    hid_block = FF // NB
    hid_sub = hid_block // NB
    upper_half = lax.Precision.HIGHEST
    kernel_blocks = jnp.moveaxis(kernel.reshape(ROOT, ROOT, NB, block_width), 2, 0)
    tap_blocks = jnp.moveaxis(short_taps, 1, 0)
    fwd_in = fwd_inner.astype(jnp.float32)
    forward_result = fwd_outer.astype(jnp.float32)
    inverse_result = inv_outer.astype(jnp.float32)
    inv_in = inv_inner.astype(jnp.float32)

    def mixer_block(portion):
        block_in, weight_in, tap_part, kernel_piece = portion
        projected = cast_bfloat16(jnp.dot(block_in, weight_in, preferred_element_type=jnp.float32)).astype(jnp.float32)
        back_one = jnp.concatenate([jnp.zeros((1, 3 * block_width), jnp.float32), projected[:-1]], 0)
        back_two = jnp.concatenate([jnp.zeros((2, 3 * block_width), jnp.float32), projected[:-2]], 0)
        mixed_all = tap_part[0] * projected + tap_part[1] * back_one + tap_part[2] * back_two
        query_part = mixed_all[:, :block_width].astype(jnp.bfloat16)
        source = (mixed_all[:, block_width:2 * block_width] * mixed_all[:, 2 * block_width:]).astype(jnp.bfloat16)
        lattice = source.astype(jnp.float32).reshape(ROOT, ROOT, block_width)
        opening_segment = cast_bfloat16(jnp.einsum('abc,bf->afc', lattice, fwd_in, precision=upper_half) * twid_inner[:, :, None]).astype(jnp.float32)
        middle_segment = cast_bfloat16(jnp.einsum('hwd,hl->lwd', opening_segment, forward_result, precision=upper_half) * kernel_piece.astype(jnp.float32)).astype(jnp.float32)
        closing_segment = cast_bfloat16(jnp.einsum('njk,nz->zjk', middle_segment, inverse_result, precision=upper_half) * backward_twiddle[:, :, None]).astype(jnp.float32)
        convolved = jnp.einsum('hfc,fe->hec', closing_segment, inv_in, precision=upper_half).reshape(SEQ_LEN, block_width)
        return (query_part.astype(jnp.float32) * convolved).astype(jnp.bfloat16)

    def mlp_rows(row_block):
        row_count = row_block.shape[0]
        row_float = row_block.astype(jnp.float32)
        sumsq = lax.optimization_barrier(jnp.sum(row_float * row_float, axis=1, keepdims=True))
        normed_mlp = (row_float * lax.rsqrt(sumsq / D + epsilon) * gain_mlp.astype(jnp.float32)).astype(jnp.bfloat16)
        upper_part = jnp.einsum('lic,ich->lih', normed_mlp.reshape(row_count, NB, block_width).astype(jnp.float32), up_blocks.astype(jnp.float32), precision=upper_half)
        active = jax.nn.gelu(upper_part).astype(jnp.bfloat16)
        permuted = jnp.transpose(active.reshape(row_count, NB, NB, hid_sub), (0, 2, 1, 3)).reshape(row_count, NB, hid_block)
        lower_part = jnp.einsum('ljk,jkd->ljd', permuted.astype(jnp.float32), down_blocks.astype(jnp.float32), precision=upper_half)
        return (row_float + lower_part.reshape(row_count, D)).astype(jnp.bfloat16)

    def one_sequence(sequence):
        seq_float = sequence.astype(jnp.float32)
        sumsq = lax.optimization_barrier(jnp.sum(seq_float * seq_float, axis=1, keepdims=True))
        normed = (seq_float * lax.rsqrt(sumsq / D + epsilon) * gain_mix.astype(jnp.float32)).astype(jnp.bfloat16)
        u_blocks = jnp.moveaxis(normed.reshape(SEQ_LEN, NB, block_width), 1, 0)
        gated_out = lax.map(mixer_block, (u_blocks, proj_in, tap_blocks, kernel_blocks))
        spread = jnp.transpose(gated_out.reshape(NB, SEQ_LEN, NB, sub_width), (1, 2, 0, 3)).reshape(SEQ_LEN, NB, block_width)
        mix_out = jnp.einsum('ljk,jkd->ljd', spread.astype(jnp.float32), proj_out.astype(jnp.float32), precision=upper_half)
        residual = (seq_float.reshape(SEQ_LEN, NB, block_width) + mix_out).astype(jnp.bfloat16).reshape(SEQ_LEN, D)
        finished = lax.map(mlp_rows, residual.reshape(8, SEQ_LEN // 8, D))
        return finished.reshape(SEQ_LEN, D)
    return lax.map(one_sequence, stream)
```

```python
import functools

import jax
import jax.numpy as jnp
from jax import lax
from jax.experimental import pallas as pl
from jax.experimental.pallas import tpu as pltpu
from jax.sharding import PartitionSpec as P

D = 1024
EPS = 1e-05
BF = jnp.bfloat16
F32 = jnp.float32
MESH = pl.DeviceIdType.MESH

SEQS = 4
TOK = 1024
CH = 128
NC = 64
NM = 8
TS = TOK // NM
STAT_ROWS = 40


def dot(a, b):
    return jnp.dot(a, b, preferred_element_type=F32)


def dot_nt(a, b):
    return lax.dot_general(a, b, (((1,), (1,)), ((), ())), preferred_element_type=F32)


def mul(v, n):
    return pl.multiple_of(v, n)


def kernel(
    x_ref,
    rim_ref,
    stat_ref,
    gain_ref,
    projin_ref,
    taps_ref,
    fi_ref,
    tw_ref,
    fo_ref,
    kern_ref,
    io_ref,
    bt_ref,
    iit_ref,
    projout_ref,
    up_ref,
    down_ref,
    out_ref,
    w1,
    w2,
    w3,
    w4,
    pw,
    upw,
    dx,
    st,
    scr,
    gain2,
    rimp,
    pj,
    src,
    q_s,
    s1,
    r1,
    sec,
    s2,
    r2,
    gt,
    g_s,
    x_s,
    h_s,
    ob,
    os_,
    st_send,
    st_recv,
    x_send,
    x_recv,
    wa_send,
    wa_recv,
    wb_send,
    wb_recv,
    c1_send,
    c1_recv,
    c2_send,
    c2_recv,
    g_send,
    g_recv,
    o_send,
    o_recv,
):
    me = lax.axis_index("ctx")
    m = lax.axis_index("mp")
    shard = (me // 16) * 2 + me % 2
    z_lo = (me // 2) % 8
    x_pos = m // 2
    z_hi = m % 2
    mate = x_pos * 2 + (1 - z_hi)

    def plane_peer(t):
        x_to = (x_pos + t // 8) % 4
        s_to = (shard + t % 8) % 8
        return (s_to // 2) * 16 + z_lo * 2 + s_to % 2, x_to * 2 + z_hi

    def remote(src_view, dst_view, send, recv, to):
        return pltpu.make_async_remote_copy(
            src_ref=src_view,
            dst_ref=dst_view,
            send_sem=send,
            recv_sem=recv,
            device_id=to,
            device_id_type=MESH,
        )

    def up_piece(b, s):
        return upw.at[b, pl.ds(mul(s * 16, 16), 16), :]

    def down_piece(b, s):
        return dx.at[
            b // 2,
            pl.ds(mul(s * 128 + (b % 2) * 64, 64), 64),
            pl.ds(mul((b % 2) * 128, 128), 128),
        ]

    def out_piece(b, s):
        return pw.at[pl.ds(mul(s * 128 + b * 16, 16), 16), pl.ds(mul(b * 128, 128), 128)]

    def clear_pw(i, c):
        pw[pl.ds(mul(i * 128, 128), 128), :] = jnp.zeros((128, 1024), BF)
        return c

    lax.fori_loop(0, 8, clear_pw, 0)

    def clear_dx(i, c):
        dx[i] = jnp.zeros((1024, 256), BF)
        return c

    lax.fori_loop(0, 4, clear_dx, 0)
    up_piece(m, shard)[...] = up_ref[pl.ds(mul(shard * 16, 16), 16), :]
    down_piece(m, shard)[...] = down_ref[pl.ds(mul(shard * 64, 64), 64), :]
    out_piece(m, shard)[...] = projout_ref[pl.ds(mul(shard * 16, 16), 16), :]
    st[m] = stat_ref[...]

    barrier = pltpu.get_barrier_semaphore()

    def greet_mp(t, c):
        pl.semaphore_signal(barrier, inc=1, device_id=(me, (m + t) % NM), device_id_type=MESH)
        return c

    lax.fori_loop(1, NM, greet_mp, 0)

    def greet_ctx(t, c):
        pl.semaphore_signal(barrier, inc=1, device_id=((me + t) % NC, m), device_id_type=MESH)
        return c

    lax.fori_loop(1, NC, greet_ctx, 0)

    def greet_plane(t, c):
        x_to = (x_pos + 1 + t // 7) % 4
        s_to = (shard + 1 + t % 7) % 8
        to = ((s_to // 2) * 16 + z_lo * 2 + s_to % 2, x_to * 2 + z_hi)
        pl.semaphore_signal(barrier, inc=1, device_id=to, device_id_type=MESH)
        return c

    lax.fori_loop(0, 21, greet_plane, 0)
    pl.semaphore_wait(barrier, (NM - 1) + (NC - 1) + 21)

    def send_stat(t, c):
        remote(st.at[m], st.at[m], st_send, st_recv, (me, (m + t) % NM)).start()
        return c

    lax.fori_loop(1, NM, send_stat, 0)
    for n, piece in enumerate((up_piece, down_piece, out_piece)):
        here = piece(m, shard)
        remote(here, here, wa_send.at[n], wa_recv.at[n], (me, mate)).start()

    def stream_copy(t):
        to = (m + t) % NM
        return remote(
            x_ref.at[:, pl.ds(mul(to * TS, TS), TS), :],
            x_s.at[:, :, pl.ds(mul(m * CH, CH), CH)],
            x_send,
            x_recv,
            (me, to),
        )

    def send_stream(t, c):
        stream_copy(t).start()
        return c

    lax.fori_loop(1, NM, send_stream, 0)
    x_s[:, :, pl.ds(mul(m * CH, CH), CH)] = x_ref[:, pl.ds(mul(m * TS, TS), TS), :]

    def build(b, c):
        rows = pl.ds(mul(b * 256, 256), 256)
        ri = b * 256 + lax.broadcasted_iota(jnp.int32, (256, 256), 0)
        ci = lax.broadcasted_iota(jnp.int32, (256, 256), 1)
        one = jnp.where(ci == (ri >> 4) * 4 + (ri & 3), 1.0, 0.0).astype(BF)
        part = dot_nt(one, fi_ref[...])
        for a in range(4):
            w1[rows, a * 256 : (a + 1) * 256] = jnp.where(((ri >> 2) & 3) == a, part, 0.0).astype(BF)
        quarter = jnp.where(ci == (ri >> 2), 1.0, 0.0).astype(BF)
        rq = lax.broadcasted_iota(jnp.int32, (256, 1024), 0)
        cq = lax.broadcasted_iota(jnp.int32, (256, 1024), 1)
        widen = jnp.where(rq == (cq >> 2), 1.0, 0.0).astype(BF)
        keep = (rq & 3) == (cq & 3)
        for factor, w in ((fo_ref, w2), (io_ref, w3)):
            part = dot_nt(quarter, factor[...]).astype(BF)
            w[rows, :] = jnp.where(keep, dot(part, widen), 0.0).astype(BF)
        pick = jnp.where(rq == (cq >> 4) * 4 + (cq & 3), 1.0, 0.0).astype(BF)
        w4[rows, :] = jnp.where(((cq >> 2) & 3) == b, dot(iit_ref[...], pick), 0.0).astype(BF)
        return c

    lax.fori_loop(0, 4, build, 0)

    remote(st.at[pl.ds(0, 7)], st.at[pl.ds(0, 7)], st_send, st_recv, (me, mate)).wait_recv()
    total = st[0]
    for b in range(1, NM):
        total = total + st[b]
    scr[...] = lax.rsqrt(total / D + EPS)
    for b in range(NM):
        gain2[:, b * CH : (b + 1) * CH] = st[b, 33:34, :]
    gain = gain_ref[...]

    def column(row):
        line = scr[pl.ds(row, 1), :]
        return jnp.transpose(jnp.broadcast_to(line, (128, 128)))

    rim_scale = column(32)[:32]
    rim_norm = (rim_ref[...].astype(F32) * rim_scale * gain).astype(BF)
    rimp[...] = dot(rim_norm, projin_ref[...]).astype(BF).astype(F32)

    def ctx_copy(t, base, out_buf, in_buf, send, recv):
        to = (me + t) % NC
        return remote(
            out_buf.at[pl.ds(mul(base + to * 16, 16), 16), :],
            in_buf.at[pl.ds(mul(base + me * 16, 16), 16), :],
            send,
            recv,
            (to, m),
        )

    def whole_ctx(base, buf, send, recv):
        view = buf.at[pl.ds(mul(base, 16), 1008), :]
        return remote(view, view, send, recv, (me, mate))

    def forward(s, c):
        base = s * TOK

        def project(b, c2):
            rows = x_ref[s, pl.ds(mul(b * 128, 128), 128), :].astype(F32)
            normed = (rows * column(s * 8 + b) * gain).astype(BF)
            pj[pl.ds(mul(8 + b * 128, 8), 128), :] = (
                dot(normed, projin_ref[...]).astype(BF).astype(F32)
            )
            return c2

        pj[0:8, :] = rimp[pl.ds(mul(s * 8, 8), 8), :]
        lax.fori_loop(0, 8, project, 0)
        for b in range(8):
            lo = b * 128
            mixed = (
                taps_ref[0:1, :] * pj[8 + lo : 136 + lo, :]
                + taps_ref[1:2, :] * pj[7 + lo : 135 + lo, :]
                + taps_ref[2:3, :] * pj[6 + lo : 134 + lo, :]
            )
            q_s[pl.ds(mul(base + lo, 128), 128), :] = mixed[:, :CH].astype(BF)
            src[lo : lo + 128, :] = (mixed[:, CH : 2 * CH] * mixed[:, 2 * CH :]).astype(BF)

        def inner(b, c2):
            rows = pl.ds(mul(b * 256, 256), 256)
            first = dot(w1[rows, :], src[...]) * tw_ref[rows, :]
            s1[pl.ds(mul(base + b * 256, 256), 256), :] = first.astype(BF)
            return c2

        lax.fori_loop(0, 4, inner, 0)

        def send(t, c2):
            ctx_copy(t, base, s1, r1, c1_send.at[s], c1_recv.at[s]).start()
            return c2

        lax.fori_loop(1, NC, send, 0)
        own = pl.ds(mul(base + me * 16, 16), 16)
        r1[own, :] = s1[own, :]
        return c

    lax.fori_loop(0, SEQS, forward, 0)

    for n, piece in enumerate((up_piece, down_piece, out_piece)):
        there = piece(mate, shard)
        remote(there, there, wa_send.at[n], wa_recv.at[n], (me, mate)).wait_recv()

    def spread_weights(t, c):
        to = plane_peer(t)
        for n, piece in enumerate((up_piece, down_piece, out_piece)):
            for b in (m, mate):
                here = piece(b, shard)
                remote(here, here, wb_send.at[n], wb_recv.at[n], to).start()
        return c

    lax.fori_loop(1, 32, spread_weights, 0)

    def middle(s, c):
        base = s * TOK
        whole_ctx(base, r1, c1_send.at[s], c1_recv.at[s]).wait_recv()

        def outer(b, c2):
            rows = pl.ds(mul(b * 256, 256), 256)
            got = r1[pl.ds(mul(base, 1024), 1024), :]
            sec[rows, :] = (dot(w2[rows, :], got) * kern_ref[rows, :].astype(F32)).astype(BF)
            return c2

        lax.fori_loop(0, 4, outer, 0)

        def back(b, c2):
            rows = pl.ds(mul(b * 256, 256), 256)
            third = dot(w3[rows, :], sec[...]) * bt_ref[rows, :]
            s2[pl.ds(mul(base + b * 256, 256), 256), :] = third.astype(BF)
            return c2

        lax.fori_loop(0, 4, back, 0)

        def send(t, c2):
            ctx_copy(t, base, s2, r2, c2_send.at[s], c2_recv.at[s]).start()
            return c2

        lax.fori_loop(1, NC, send, 0)
        own = pl.ds(mul(base + me * 16, 16), 16)
        r2[own, :] = s2[own, :]
        return c

    lax.fori_loop(0, SEQS, middle, 0)

    def gate(s, c):
        base = s * TOK
        whole_ctx(base, r2, c2_send.at[s], c2_recv.at[s]).wait_recv()

        def last(b, c2):
            rows = pl.ds(mul(b * 256, 256), 256)
            here = pl.ds(mul(base + b * 256, 256), 256)
            conv = dot(w4[rows, :], r2[pl.ds(mul(base, 1024), 1024), :])
            gt[here, :] = (q_s[here, :].astype(F32) * conv).astype(BF)
            return c2

        lax.fori_loop(0, 4, last, 0)

        def send(t, c2):
            to = (m + t) % NM
            remote(
                gt.at[pl.ds(mul(base + to * TS, TS), TS), :],
                g_s.at[s, :, pl.ds(mul(m * CH, CH), CH)],
                g_send.at[s],
                g_recv.at[s],
                (me, to),
            ).start()
            return c2

        lax.fori_loop(1, NM, send, 0)
        g_s[s, :, pl.ds(mul(m * CH, CH), CH)] = gt[pl.ds(mul(base + m * TS, TS), TS), :]
        return c

    lax.fori_loop(0, SEQS, gate, 0)

    up_all = r1.at[pl.ds(0, 62 * 64), :]
    out_all = r1.at[pl.ds(0, 62 * 16), :]
    for n, view in enumerate((up_all, up_all, out_all)):
        remote(view, view, wb_send.at[n], wb_recv.at[n], (me, mate)).wait_recv()
    x_all = x_s.at[:, :, pl.ds(0, 7 * CH)]
    remote(x_all, x_all, x_send, x_recv, (me, mate)).wait_recv()

    def finish(s, c):
        g_all = g_s.at[s, :, pl.ds(0, 7 * CH)]
        remote(g_all, g_all, g_send.at[s], g_recv.at[s], (me, mate)).wait_recv()
        resid = (x_s[s].astype(F32) + dot(g_s[s], pw[...])).astype(BF).astype(F32)
        sumsq = jnp.sum(resid * resid, axis=1, keepdims=True)
        normed = (resid * lax.rsqrt(sumsq / D + EPS) * gain2[...]).astype(BF)
        for i in range(NM):
            act = jax.nn.gelu(dot(normed[:, i * CH : (i + 1) * CH], upw[i])).astype(BF)
            for jj in range(4):
                h_s[jj, :, i * 128 : (i + 1) * 128] = act[:, jj * 128 : (jj + 1) * 128]
        for jj in range(4):
            low = dot(h_s[jj], dx[jj]) + resid[:, jj * 256 : (jj + 1) * 256]
            ob[s, 2 * jj] = low[:, :CH].astype(BF)
            ob[s, 2 * jj + 1] = low[:, CH:].astype(BF)

        rows = pl.ds(mul(s * TOK + m * TS, TS), TS)

        def send(t, c2):
            to = (m + t) % NM
            remote(ob.at[s, to], os_.at[rows, :], o_send, o_recv, (me, to)).start()
            return c2

        lax.fori_loop(1, NM, send, 0)
        os_[rows, :] = ob[s, m]
        return c

    lax.fori_loop(0, SEQS, finish, 0)

    o_all = os_.at[pl.ds(0, 28 * TS), :]
    remote(o_all, o_all, o_send, o_recv, (me, mate)).wait()
    remote(st.at[pl.ds(0, 7)], st.at[pl.ds(0, 7)], st_send, st_recv, (me, mate)).wait_send()
    for n, piece in enumerate((up_piece, down_piece, out_piece)):
        here = piece(m, shard)
        remote(here, here, wa_send.at[n], wa_recv.at[n], (me, mate)).wait_send()
    for n, view in enumerate((up_all, up_all, out_all)):
        remote(view, view, wb_send.at[n], wb_recv.at[n], (me, mate)).wait_send()
    remote(x_all, x_all, x_send, x_recv, (me, mate)).wait_send()

    def drain(s, c):
        base = s * TOK
        whole_ctx(base, s1, c1_send.at[s], c1_recv.at[s]).wait_send()
        whole_ctx(base, s2, c2_send.at[s], c2_recv.at[s]).wait_send()
        g_all = g_s.at[s, :, pl.ds(0, 7 * CH)]
        remote(g_all, g_all, g_send.at[s], g_recv.at[s], (me, mate)).wait_send()
        return c

    lax.fori_loop(0, SEQS, drain, 0)
    out_ref[...] = os_[...]


def body(
    stream,
    gain_mix,
    proj_in,
    short_taps,
    fwd_inner,
    twid_inner,
    fwd_outer,
    kernel_grid,
    inv_outer,
    backward_twiddle,
    inv_inner,
    proj_out,
    gain_mlp,
    up_blocks,
    down_blocks,
):
    pairs = [(i, i + 1) for i in range(NC - 1)]
    rim = lax.ppermute(stream[:, TOK - 8 :, :], "ctx", pairs)
    x_float = stream.astype(F32)
    rim_float = rim.astype(F32)
    sums = jnp.sum(x_float * x_float, axis=2).reshape(32, 128)
    rim_sums = jnp.sum(rim_float * rim_float, axis=2).reshape(1, 32)
    stats = jnp.concatenate(
        [
            sums,
            jnp.pad(rim_sums, ((0, 0), (0, 96))),
            gain_mlp.astype(F32).reshape(1, CH),
            jnp.zeros((STAT_ROWS - 34, 128), F32),
        ],
        axis=0,
    )
    tw = twid_inner.reshape(4, NC, 4).transpose(1, 0, 2).reshape(TOK, 1)
    bt = backward_twiddle.reshape(TOK, 1)
    operands = (
        stream,
        rim.reshape(32, CH),
        stats,
        gain_mix.astype(F32).reshape(1, CH),
        proj_in[0],
        short_taps[:, 0, :],
        fwd_inner,
        tw,
        fwd_outer,
        kernel_grid.reshape(TOK, CH),
        inv_outer,
        bt,
        inv_inner.T,
        proj_out[0],
        up_blocks[0],
        down_blocks[0],
    )
    vmem = pl.BlockSpec(memory_space=pltpu.VMEM)
    dma = pltpu.SemaphoreType.DMA
    flat = pltpu.VMEM((SEQS * TOK, CH), BF)
    square = pltpu.VMEM((1024, 1024), BF)
    out = pl.pallas_call(
        kernel,
        out_shape=jax.ShapeDtypeStruct((SEQS * TOK, CH), BF),
        in_specs=[vmem] * len(operands),
        out_specs=vmem,
        scratch_shapes=[
            square,
            square,
            square,
            square,
            square,
            pltpu.VMEM((NM, CH, 512), BF),
            pltpu.VMEM((4, 1024, 256), BF),
            pltpu.VMEM((NM, STAT_ROWS, 128), F32),
            pltpu.VMEM((STAT_ROWS, 128), F32),
            pltpu.VMEM((1, 1024), F32),
            pltpu.VMEM((32, 3 * CH), F32),
            pltpu.VMEM((8 + TOK, 3 * CH), F32),
            pltpu.VMEM((TOK, CH), BF),
            flat,
            flat,
            flat,
            pltpu.VMEM((TOK, CH), BF),
            flat,
            flat,
            flat,
            pltpu.VMEM((SEQS, TS, 1024), BF),
            pltpu.VMEM((SEQS, TS, 1024), BF),
            pltpu.VMEM((4, TS, 1024), BF),
            pltpu.VMEM((SEQS, NM, TS, CH), BF),
            flat,
            dma,
            dma,
            dma,
            dma,
            dma((3,)),
            dma((3,)),
            dma((3,)),
            dma((3,)),
            dma((SEQS,)),
            dma((SEQS,)),
            dma((SEQS,)),
            dma((SEQS,)),
            dma((SEQS,)),
            dma((SEQS,)),
            dma,
            dma,
        ],
        compiler_params=pltpu.CompilerParams(
            collective_id=0, has_side_effects=True, vmem_limit_bytes=60 * 1024 * 1024
        ),
        name="monarch_block",
    )(*operands)
    return out.reshape(SEQS, TOK, CH)


def solution(mesh):
    placed = (
        P(None, "ctx", "mp"),
        P("mp"),
        P("mp", None, None),
        P(None, "mp", None),
        P(),
        P("ctx", None),
        P(),
        P(None, "ctx", "mp"),
        P(),
        P(None, "ctx"),
        P(),
        P("mp", None, None),
        P("mp"),
        P("mp", None, None),
        P("mp", None, None),
    )
    return jax.shard_map(
        body, mesh=mesh, in_specs=placed, out_specs=P(None, "ctx", "mp"), check_vma=False
    )
```

```python
import functools

import jax
import jax.numpy as jnp
from jax import lax
from jax.experimental import pallas as pl
from jax.experimental.pallas import tpu as pltpu
from jax.sharding import PartitionSpec as P

D = 1024
EPS = 1e-05
BF = jnp.bfloat16
F32 = jnp.float32
MESH = pl.DeviceIdType.MESH

SEQS = 4
TOK = 1024
CH = 128
NC = 64
NM = 8
TS = TOK // NM
STAT_ROWS = 40


def dot(a, b):
    return jnp.dot(a, b, preferred_element_type=F32)


def dot_nt(a, b):
    return lax.dot_general(a, b, (((1,), (1,)), ((), ())), preferred_element_type=F32)


def mul(v, n):
    return pl.multiple_of(v, n)


def kernel(
    x_ref,
    gain_ref,
    projin_ref,
    taps_ref,
    fi_ref,
    tw_ref,
    fo_ref,
    kern_ref,
    io_ref,
    bt_ref,
    ii_ref,
    projout_ref,
    up_ref,
    down_ref,
    out_ref,
    w1,
    w2,
    w3,
    w4,
    pw,
    upw,
    dx,
    st,
    rt,
    rr,
    rimx,
    twb,
    btb,
    scr,
    gain2,
    rimp,
    pj,
    src,
    q_s,
    s1,
    r1,
    sec,
    s2,
    r2,
    gt,
    g_s,
    x_s,
    h_s,
    ob,
    os_,
    st_send,
    st_recv,
    x_send,
    x_recv,
    wa_send,
    wa_recv,
    wb_send,
    wb_recv,
    ws_send,
    ws_recv,
    rt_send,
    rt_recv,
    rx_send,
    rx_recv,
    c1_send,
    c1_recv,
    c2_send,
    c2_recv,
    g_send,
    g_recv,
    o_send,
    o_recv,
):
    me = lax.axis_index("ctx")
    m = lax.axis_index("mp")
    core = me % 2
    y_pos = me // 16
    z_lo = (me // 2) % 8
    shard = core * 4 + y_pos
    x_pos = m // 2
    z_hi = m % 2
    mate = x_pos * 2 + (1 - z_hi)
    twin = me + 1 - 2 * core
    after = (me + 1) % NC
    before = (me + NC - 1) % NC

    def plane_peer(t):
        x_to = (x_pos + t // 4) % 4
        y_to = (y_pos + t % 4) % 4
        return y_to * 16 + z_lo * 2 + core, x_to * 2 + z_hi

    def remote(src_view, dst_view, send, recv, to):
        return pltpu.make_async_remote_copy(
            src_ref=src_view,
            dst_ref=dst_view,
            send_sem=send,
            recv_sem=recv,
            device_id=to,
            device_id_type=MESH,
        )

    def up_piece(b, s):
        return upw.at[b, pl.ds(mul(s * 16, 16), 16), :]

    def down_piece(b, s):
        return dx.at[
            b // 2,
            pl.ds(mul(s * 128 + (b % 2) * 64, 64), 64),
            pl.ds(mul((b % 2) * 128, 128), 128),
        ]

    def out_piece(b, s):
        return pw.at[pl.ds(mul(s * 128 + b * 16, 16), 16), pl.ds(mul(b * 128, 128), 128)]

    def clear_pw(i, c):
        pw[pl.ds(mul(i * 128, 128), 128), :] = jnp.zeros((128, 1024), BF)
        return c

    lax.fori_loop(0, 8, clear_pw, 0)

    def clear_dx(i, c):
        dx[i] = jnp.zeros((1024, 256), BF)
        return c

    lax.fori_loop(0, 4, clear_dx, 0)
    barrier = pltpu.get_barrier_semaphore()

    def greet_mp(t, c):
        pl.semaphore_signal(barrier, inc=1, device_id=(me, (m + t) % NM), device_id_type=MESH)
        return c

    lax.fori_loop(1, NM, greet_mp, 0)

    def greet_ctx(t, c):
        pl.semaphore_signal(barrier, inc=1, device_id=((me + t) % NC, m), device_id_type=MESH)
        return c

    lax.fori_loop(1, NC, greet_ctx, 0)

    def greet_plane(t, c):
        to = plane_peer(4 * (1 + t // 3) + 1 + t % 3)
        pl.semaphore_signal(barrier, inc=1, device_id=to, device_id_type=MESH)
        return c

    lax.fori_loop(0, 9, greet_plane, 0)

    def greet_rim(t, c):
        to = (m + t) % NM
        pl.semaphore_signal(barrier, inc=1, device_id=(after, to), device_id_type=MESH)
        pl.semaphore_signal(barrier, inc=1, device_id=(before, to), device_id_type=MESH)
        return c

    lax.fori_loop(1, NM, greet_rim, 0)

    up_piece(m, shard)[...] = up_ref[pl.ds(mul(shard * 16, 16), 16), :]
    down_piece(m, shard)[...] = down_ref[pl.ds(mul(shard * 64, 64), 64), :]
    out_piece(m, shard)[...] = projout_ref[pl.ds(mul(shard * 16, 16), 16), :]
    ones = jnp.ones((8, CH), BF)
    rt[...] = jnp.zeros((8, 128), F32)
    st[m, 32:40, :] = jnp.broadcast_to(gain_ref[1:2, :], (8, 128))

    def sums(s, c):
        for b in range(8):
            rows = x_ref[s, b * 128 : (b + 1) * 128, :].astype(F32)
            square = rows * rows
            high = square.astype(BF)
            low = (square - high.astype(F32)).astype(BF)
            line = (dot_nt(ones, high) + dot_nt(ones, low))[0:1]
            st[m, pl.ds(s * 8 + b, 1), :] = line
            if b == 7:
                rt[pl.ds(s, 1), :] = line
        return c

    lax.fori_loop(0, SEQS, sums, 0)
    pl.semaphore_wait(barrier, (NM - 1) + (NC - 1) + 9 + 2 * (NM - 1))

    def send_stat(t, c):
        remote(st.at[m], st.at[m], st_send, st_recv, (me, (m + t) % NM)).start()
        return c

    lax.fori_loop(1, NM, send_stat, 0)

    def send_rim(t, c):
        remote(rt, rr.at[m], rt_send, rt_recv, (after, (m + t) % NM)).start()
        return c

    lax.fori_loop(0, NM, send_rim, 0)
    remote(x_ref.at[:, pl.ds(TOK - 16, 16), :], rimx, rx_send, rx_recv, (after, m)).start()
    for n, piece in enumerate((up_piece, down_piece, out_piece)):
        here = piece(m, shard)
        remote(here, here, wa_send.at[n], wa_recv.at[n], (me, mate)).start()

    def spread(block):
        def send(t, c):
            for n, piece in enumerate((up_piece, down_piece, out_piece)):
                here = piece(block, shard)
                remote(here, here, wb_send.at[n], wb_recv.at[n], plane_peer(t)).start()
            return c

        lax.fori_loop(1, 16, send, 0)

    spread(m)

    def stream_copy(t):
        to = (m + t) % NM
        return remote(
            x_ref.at[:, pl.ds(mul(to * TS, TS), TS), :],
            x_s.at[:, :, pl.ds(mul(m * CH, CH), CH)],
            x_send,
            x_recv,
            (me, to),
        )

    def send_stream(t, c):
        stream_copy(t).start()
        return c

    lax.fori_loop(1, NM, send_stream, 0)
    x_s[:, :, pl.ds(mul(m * CH, CH), CH)] = x_ref[:, pl.ds(mul(m * TS, TS), TS), :]

    eye_r = lax.broadcasted_iota(jnp.int32, (256, 256), 0)
    eye_c = lax.broadcasted_iota(jnp.int32, (256, 256), 1)
    turned = dot_nt(jnp.where(eye_r == eye_c, 1.0, 0.0).astype(BF), ii_ref[...]).astype(BF)

    def build(b, c):
        rows = pl.ds(mul(b * 256, 256), 256)
        ri = b * 256 + lax.broadcasted_iota(jnp.int32, (256, 256), 0)
        ci = lax.broadcasted_iota(jnp.int32, (256, 256), 1)
        one = jnp.where(ci == (ri >> 4) * 4 + (ri & 3), 1.0, 0.0).astype(BF)
        part = dot_nt(one, fi_ref[...])
        for a in range(4):
            w1[rows, a * 256 : (a + 1) * 256] = jnp.where(((ri >> 2) & 3) == a, part, 0.0).astype(BF)
        quarter = jnp.where(ci == (ri >> 2), 1.0, 0.0).astype(BF)
        lane = lax.broadcasted_iota(jnp.int32, (256, 4), 1)
        row = b * 256 + lax.broadcasted_iota(jnp.int32, (256, 4), 0)
        for hot, factor, which, to in (
            (one, tw_ref, (row >> 2) & 3, twb),
            (quarter, bt_ref, row & 3, btb),
        ):
            part = lax.dot_general(
                hot.astype(F32),
                factor[...],
                (((1,), (1,)), ((), ())),
                precision=lax.Precision.HIGHEST,
                preferred_element_type=F32,
            )
            line = jnp.sum(jnp.where(lane == which, part, 0.0), axis=1, keepdims=True)
            to[rows, :] = jnp.broadcast_to(line, (256, 128))
        rq = lax.broadcasted_iota(jnp.int32, (256, 1024), 0)
        cq = lax.broadcasted_iota(jnp.int32, (256, 1024), 1)
        widen = jnp.where(rq == (cq >> 2), 1.0, 0.0).astype(BF)
        keep = (rq & 3) == (cq & 3)
        for factor, w in ((fo_ref, w2), (io_ref, w3)):
            part = dot_nt(quarter, factor[...]).astype(BF)
            w[rows, :] = jnp.where(keep, dot(part, widen), 0.0).astype(BF)
        pick = jnp.where(rq == (cq >> 4) * 4 + (cq & 3), 1.0, 0.0).astype(BF)
        w4[rows, :] = jnp.where(((cq >> 2) & 3) == b, dot(turned, pick), 0.0).astype(BF)
        return c

    lax.fori_loop(0, 4, build, 0)

    remote(st.at[pl.ds(0, 7)], st.at[pl.ds(0, 7)], st_send, st_recv, (me, mate)).wait_recv()
    total = st[0]
    for b in range(1, NM):
        total = total + st[b]
    scr[0:STAT_ROWS, :] = lax.rsqrt(total / D + EPS)
    for b in range(NM):
        gain2[:, b * CH : (b + 1) * CH] = st[b, 32:33, :]
    gain = gain_ref[0:1, :]

    def column(row):
        line = scr[pl.ds(row, 1), :]
        return jnp.transpose(jnp.broadcast_to(line, (128, 128)))

    remote(rr, rr, rt_send, rt_recv, (me, mate)).wait_recv()
    remote(rimx, rimx, rx_send, rx_recv, (me, mate)).wait_recv()
    total = rr[0]
    for b in range(1, NM):
        total = total + rr[b]
    scr[STAT_ROWS : STAT_ROWS + 8, :] = lax.rsqrt(total / D + EPS)
    for s in range(SEQS):
        rows = rimx[s].astype(F32)[8:16] * column(STAT_ROWS + s)[120:128] * gain
        edge = dot(jnp.concatenate([rows, rows], 0).astype(BF), projin_ref[...])[:8]
        edge = edge.astype(BF).astype(F32)
        rimp[s * 8 : s * 8 + 8, :] = jnp.where(me > 0, edge, 0.0)

    def ctx_copy(t, base, out_buf, in_buf, send, recv):
        to = (me + t) % NC
        return remote(
            out_buf.at[pl.ds(mul(base + to * 16, 16), 16), :],
            in_buf.at[pl.ds(mul(base + me * 16, 16), 16), :],
            send,
            recv,
            (to, m),
        )

    def whole_ctx(base, buf, send, recv):
        view = buf.at[pl.ds(mul(base, 16), 1008), :]
        return remote(view, view, send, recv, (me, mate))

    def forward(s, c):
        base = s * TOK

        def project(b, c2):
            rows = x_ref[s, pl.ds(mul(b * 128, 128), 128), :].astype(F32)
            normed = (rows * column(s * 8 + b) * gain).astype(BF)
            pj[pl.ds(mul(8 + b * 128, 8), 128), :] = (
                dot(normed, projin_ref[...]).astype(BF).astype(F32)
            )
            return c2

        pj[0:8, :] = rimp[pl.ds(mul(s * 8, 8), 8), :]
        lax.fori_loop(0, 8, project, 0)
        for b in range(8):
            lo = b * 128
            mixed = (
                taps_ref[0] * pj[8 + lo : 136 + lo, :]
                + taps_ref[1] * pj[7 + lo : 135 + lo, :]
                + taps_ref[2] * pj[6 + lo : 134 + lo, :]
            )
            q_s[pl.ds(mul(base + lo, 128), 128), :] = mixed[:, :CH].astype(BF)
            src[lo : lo + 128, :] = (mixed[:, CH : 2 * CH] * mixed[:, 2 * CH :]).astype(BF)

        def inner(b, c2):
            rows = pl.ds(mul(b * 256, 256), 256)
            first = dot(w1[rows, :], src[...]) * twb[rows, :]
            s1[pl.ds(mul(base + b * 256, 256), 256), :] = first.astype(BF)
            return c2

        lax.fori_loop(0, 4, inner, 0)

        def send(t, c2):
            ctx_copy(t, base, s1, r1, c1_send.at[s], c1_recv.at[s]).start()
            return c2

        lax.fori_loop(1, NC, send, 0)
        own = pl.ds(mul(base + me * 16, 16), 16)
        r1[own, :] = s1[own, :]

        @pl.when(s == 0)
        def _():
            for n, piece in enumerate((up_piece, down_piece, out_piece)):
                there = piece(mate, shard)
                remote(there, there, wa_send.at[n], wa_recv.at[n], (me, mate)).wait_recv()
            spread(mate)

        return c

    lax.fori_loop(0, SEQS, forward, 0)

    up_all = r1.at[pl.ds(0, 30 * 64), :]
    out_all = r1.at[pl.ds(0, 30 * 16), :]
    for n, view in enumerate((up_all, up_all, out_all)):
        remote(view, view, wb_send.at[n], wb_recv.at[n], (me, mate)).wait_recv()

    def halves(side):
        return (
            upw.at[:, pl.ds(mul(side * 64, 64), 64), :],
            dx.at[:, pl.ds(mul(side * 512, 512), 512), :],
            pw.at[pl.ds(mul(side * 512, 512), 512), :],
        )

    for n, half in enumerate(halves(core)):
        remote(half, half, ws_send.at[n], ws_recv.at[n], (twin, m)).start()

    def middle(s, c):
        base = s * TOK
        whole_ctx(base, r1, c1_send.at[s], c1_recv.at[s]).wait_recv()

        def outer(b, c2):
            rows = pl.ds(mul(b * 256, 256), 256)
            got = r1[pl.ds(mul(base, 1024), 1024), :]
            sec[rows, :] = (dot(w2[rows, :], got) * kern_ref[rows, :].astype(F32)).astype(BF)
            return c2

        lax.fori_loop(0, 4, outer, 0)

        def back(b, c2):
            rows = pl.ds(mul(b * 256, 256), 256)
            third = dot(w3[rows, :], sec[...]) * btb[rows, :]
            s2[pl.ds(mul(base + b * 256, 256), 256), :] = third.astype(BF)
            return c2

        lax.fori_loop(0, 4, back, 0)

        def send(t, c2):
            ctx_copy(t, base, s2, r2, c2_send.at[s], c2_recv.at[s]).start()
            return c2

        lax.fori_loop(1, NC, send, 0)
        own = pl.ds(mul(base + me * 16, 16), 16)
        r2[own, :] = s2[own, :]
        return c

    lax.fori_loop(0, SEQS, middle, 0)

    def gate(s, c):
        base = s * TOK
        whole_ctx(base, r2, c2_send.at[s], c2_recv.at[s]).wait_recv()

        def last(b, c2):
            rows = pl.ds(mul(b * 256, 256), 256)
            here = pl.ds(mul(base + b * 256, 256), 256)
            conv = dot(w4[rows, :], r2[pl.ds(mul(base, 1024), 1024), :])
            gt[here, :] = (q_s[here, :].astype(F32) * conv).astype(BF)
            return c2

        lax.fori_loop(0, 4, last, 0)

        def send(t, c2):
            to = (m + t) % NM
            remote(
                gt.at[pl.ds(mul(base + to * TS, TS), TS), :],
                g_s.at[s, :, pl.ds(mul(m * CH, CH), CH)],
                g_send.at[s],
                g_recv.at[s],
                (me, to),
            ).start()
            return c2

        lax.fori_loop(1, NM, send, 0)
        g_s[s, :, pl.ds(mul(m * CH, CH), CH)] = gt[pl.ds(mul(base + m * TS, TS), TS), :]
        return c

    lax.fori_loop(0, SEQS, gate, 0)

    for n, half in enumerate(halves(1 - core)):
        remote(half, half, ws_send.at[n], ws_recv.at[n], (twin, m)).wait_recv()
    x_all = x_s.at[:, :, pl.ds(0, 7 * CH)]
    remote(x_all, x_all, x_send, x_recv, (me, mate)).wait_recv()

    def finish(s, c):
        g_all = g_s.at[s, :, pl.ds(0, 7 * CH)]
        remote(g_all, g_all, g_send.at[s], g_recv.at[s], (me, mate)).wait_recv()
        resid = (x_s[s].astype(F32) + dot(g_s[s], pw[...])).astype(BF).astype(F32)
        sumsq = jnp.sum(resid * resid, axis=1, keepdims=True)
        normed = (resid * lax.rsqrt(sumsq / D + EPS) * gain2[...]).astype(BF)
        for i in range(NM):
            act = jax.nn.gelu(dot(normed[:, i * CH : (i + 1) * CH], upw[i])).astype(BF)
            for jj in range(4):
                h_s[jj, :, i * 128 : (i + 1) * 128] = act[:, jj * 128 : (jj + 1) * 128]
        for jj in range(4):
            low = dot(h_s[jj], dx[jj]) + resid[:, jj * 256 : (jj + 1) * 256]
            ob[s, 2 * jj] = low[:, :CH].astype(BF)
            ob[s, 2 * jj + 1] = low[:, CH:].astype(BF)

        rows = pl.ds(mul(s * TOK + m * TS, TS), TS)

        def send(t, c2):
            to = (m + t) % NM
            remote(ob.at[s, to], os_.at[rows, :], o_send, o_recv, (me, to)).start()
            return c2

        lax.fori_loop(1, NM, send, 0)
        os_[rows, :] = ob[s, m]
        return c

    lax.fori_loop(0, SEQS, finish, 0)

    o_all = os_.at[pl.ds(0, 28 * TS), :]
    remote(o_all, o_all, o_send, o_recv, (me, mate)).wait()
    remote(st.at[pl.ds(0, 7)], st.at[pl.ds(0, 7)], st_send, st_recv, (me, mate)).wait_send()
    for n, piece in enumerate((up_piece, down_piece, out_piece)):
        here = piece(m, shard)
        remote(here, here, wa_send.at[n], wa_recv.at[n], (me, mate)).wait_send()
    for n, view in enumerate((up_all, up_all, out_all)):
        remote(view, view, wb_send.at[n], wb_recv.at[n], (me, mate)).wait_send()
    remote(x_all, x_all, x_send, x_recv, (me, mate)).wait_send()
    for n, half in enumerate(halves(core)):
        remote(half, half, ws_send.at[n], ws_recv.at[n], (twin, m)).wait_send()
    remote(rr, rr, rt_send, rt_recv, (me, mate)).wait_send()
    remote(rimx, rimx, rx_send, rx_recv, (me, mate)).wait_send()

    def drain(s, c):
        base = s * TOK
        whole_ctx(base, s1, c1_send.at[s], c1_recv.at[s]).wait_send()
        whole_ctx(base, s2, c2_send.at[s], c2_recv.at[s]).wait_send()
        g_all = g_s.at[s, :, pl.ds(0, 7 * CH)]
        remote(g_all, g_all, g_send.at[s], g_recv.at[s], (me, mate)).wait_send()
        return c

    lax.fori_loop(0, SEQS, drain, 0)
    out_ref[...] = os_[...]


def body(
    stream,
    gain_mix,
    proj_in,
    short_taps,
    fwd_inner,
    twid_inner,
    fwd_outer,
    kernel_grid,
    inv_outer,
    backward_twiddle,
    inv_inner,
    proj_out,
    gain_mlp,
    up_blocks,
    down_blocks,
):
    gains = jnp.stack([gain_mix, gain_mlp]).astype(F32)
    operands = (
        stream,
        gains,
        proj_in[0],
        short_taps,
        fwd_inner,
        twid_inner,
        fwd_outer,
        kernel_grid.reshape(TOK, CH),
        inv_outer,
        backward_twiddle.T,
        inv_inner,
        proj_out[0],
        up_blocks[0],
        down_blocks[0],
    )
    vmem = pl.BlockSpec(memory_space=pltpu.VMEM)
    dma = pltpu.SemaphoreType.DMA
    flat = pltpu.VMEM((SEQS * TOK, CH), BF)
    square = pltpu.VMEM((1024, 1024), BF)
    out = pl.pallas_call(
        kernel,
        out_shape=jax.ShapeDtypeStruct((SEQS * TOK, CH), BF),
        in_specs=[vmem] * len(operands),
        out_specs=vmem,
        scratch_shapes=[
            square,
            square,
            square,
            square,
            square,
            pltpu.VMEM((NM, CH, 512), BF),
            pltpu.VMEM((4, 1024, 256), BF),
            pltpu.VMEM((NM, STAT_ROWS, 128), F32),
            pltpu.VMEM((8, 128), F32),
            pltpu.VMEM((NM, 8, 128), F32),
            pltpu.VMEM((SEQS, 16, CH), BF),
            pltpu.VMEM((TOK, 128), F32),
            pltpu.VMEM((TOK, 128), F32),
            pltpu.VMEM((STAT_ROWS + 8, 128), F32),
            pltpu.VMEM((1, 1024), F32),
            pltpu.VMEM((32, 3 * CH), F32),
            pltpu.VMEM((8 + TOK, 3 * CH), F32),
            pltpu.VMEM((TOK, CH), BF),
            flat,
            flat,
            flat,
            pltpu.VMEM((TOK, CH), BF),
            flat,
            flat,
            flat,
            pltpu.VMEM((SEQS, TS, 1024), BF),
            pltpu.VMEM((SEQS, TS, 1024), BF),
            pltpu.VMEM((4, TS, 1024), BF),
            pltpu.VMEM((SEQS, NM, TS, CH), BF),
            flat,
            dma,
            dma,
            dma,
            dma,
            dma((3,)),
            dma((3,)),
            dma((3,)),
            dma((3,)),
            dma((3,)),
            dma((3,)),
            dma,
            dma,
            dma,
            dma,
            dma((SEQS,)),
            dma((SEQS,)),
            dma((SEQS,)),
            dma((SEQS,)),
            dma((SEQS,)),
            dma((SEQS,)),
            dma,
            dma,
        ],
        compiler_params=pltpu.CompilerParams(
            collective_id=0, has_side_effects=True, vmem_limit_bytes=60 * 1024 * 1024
        ),
        name="monarch_block",
    )(*operands)
    return out.reshape(SEQS, TOK, CH)


def solution(mesh):
    placed = (
        P(None, "ctx", "mp"),
        P("mp"),
        P("mp", None, None),
        P(None, "mp", None),
        P(),
        P("ctx", None),
        P(),
        P(None, "ctx", "mp"),
        P(),
        P(None, "ctx"),
        P(),
        P("mp", None, None),
        P("mp"),
        P("mp", None, None),
        P("mp", None, None),
    )
    return jax.shard_map(
        body, mesh=mesh, in_specs=placed, out_specs=P(None, "ctx", "mp"), check_vma=False
    )
```

```python
import functools

import jax
import jax.numpy as jnp
from jax import lax
from jax.experimental import pallas as pl
from jax.experimental.pallas import tpu as pltpu
from jax.sharding import PartitionSpec as P

D = 1024
EPS = 1e-05
BF = jnp.bfloat16
F32 = jnp.float32
MESH = pl.DeviceIdType.MESH

SEQS = 4
TOK = 1024
CH = 128
NC = 64
NM = 8
TS = TOK // NM
STAT_ROWS = 40


def dot(a, b):
    return jnp.dot(a, b, preferred_element_type=F32)


def dot_nt(a, b):
    return lax.dot_general(a, b, (((1,), (1,)), ((), ())), preferred_element_type=F32)


def mul(v, n):
    return pl.multiple_of(v, n)


def kernel(
    x_ref,
    gain_ref,
    projin_ref,
    taps_ref,
    fi_ref,
    tw_ref,
    fo_ref,
    kern_ref,
    io_ref,
    bt_ref,
    ii_ref,
    projout_ref,
    up_ref,
    down_ref,
    out_ref,
    w1,
    w2,
    w3,
    w4,
    pw,
    upw,
    dx,
    st,
    rt,
    rr,
    rimx,
    twb,
    btb,
    scr,
    gain2,
    rimp,
    pj,
    src,
    q_s,
    s1,
    r1,
    sec,
    s2,
    r2,
    gt,
    g_s,
    x_s,
    h_s,
    ob,
    os_,
    st_send,
    st_recv,
    x_send,
    x_recv,
    wa_send,
    wa_recv,
    wb_send,
    wb_recv,
    ws_send,
    ws_recv,
    rt_send,
    rt_recv,
    rx_send,
    rx_recv,
    c1_send,
    c1_recv,
    c2_send,
    c2_recv,
    g_send,
    g_recv,
    o_send,
    o_recv,
):
    me = lax.axis_index("ctx")
    m = lax.axis_index("mp")
    core = me % 2
    y_pos = me // 16
    z_lo = (me // 2) % 8
    shard = core * 4 + y_pos
    x_pos = m // 2
    z_hi = m % 2
    mate = x_pos * 2 + (1 - z_hi)
    twin = me + 1 - 2 * core
    after = (me + 1) % NC
    before = (me + NC - 1) % NC

    def plane_peer(t):
        x_to = (x_pos + t // 4) % 4
        y_to = (y_pos + t % 4) % 4
        return y_to * 16 + z_lo * 2 + core, x_to * 2 + z_hi

    def remote(src_view, dst_view, send, recv, to):
        return pltpu.make_async_remote_copy(
            src_ref=src_view,
            dst_ref=dst_view,
            send_sem=send,
            recv_sem=recv,
            device_id=to,
            device_id_type=MESH,
        )

    def up_piece(b, s):
        return upw.at[b, pl.ds(mul(s * 16, 16), 16), :]

    def down_piece(b, s):
        return dx.at[
            b // 2,
            pl.ds(mul(s * 128 + (b % 2) * 64, 64), 64),
            pl.ds(mul((b % 2) * 128, 128), 128),
        ]

    def out_piece(b, s):
        return pw.at[pl.ds(mul(s * 128 + b * 16, 16), 16), pl.ds(mul(b * 128, 128), 128)]

    def clear_pw(i, c):
        pw[pl.ds(mul(i * 128, 128), 128), :] = jnp.zeros((128, 1024), BF)
        return c

    lax.fori_loop(0, 8, clear_pw, 0)

    def clear_dx(i, c):
        dx[i] = jnp.zeros((1024, 256), BF)
        return c

    lax.fori_loop(0, 4, clear_dx, 0)
    barrier = pltpu.get_barrier_semaphore()

    def greet_mp(t, c):
        pl.semaphore_signal(barrier, inc=1, device_id=(me, (m + t) % NM), device_id_type=MESH)
        return c

    lax.fori_loop(1, NM, greet_mp, 0)

    def greet_ctx(t, c):
        pl.semaphore_signal(barrier, inc=1, device_id=((me + t) % NC, m), device_id_type=MESH)
        return c

    lax.fori_loop(1, NC, greet_ctx, 0)

    def greet_plane(t, c):
        to = plane_peer(4 * (1 + t // 3) + 1 + t % 3)
        pl.semaphore_signal(barrier, inc=1, device_id=to, device_id_type=MESH)
        return c

    lax.fori_loop(0, 9, greet_plane, 0)

    def greet_rim(t, c):
        to = (m + t) % NM
        pl.semaphore_signal(barrier, inc=1, device_id=(after, to), device_id_type=MESH)
        pl.semaphore_signal(barrier, inc=1, device_id=(before, to), device_id_type=MESH)
        return c

    lax.fori_loop(1, NM, greet_rim, 0)

    up_piece(m, shard)[...] = up_ref[pl.ds(mul(shard * 16, 16), 16), :]
    down_piece(m, shard)[...] = down_ref[pl.ds(mul(shard * 64, 64), 64), :]
    out_piece(m, shard)[...] = projout_ref[pl.ds(mul(shard * 16, 16), 16), :]
    ones = jnp.ones((8, CH), BF)
    rt[...] = jnp.zeros((8, 128), F32)
    st[m, 32:40, :] = jnp.broadcast_to(gain_ref[1:2, :], (8, 128))

    def sums(s, c):
        for b in range(8):
            rows = x_ref[s, b * 128 : (b + 1) * 128, :].astype(F32)
            square = rows * rows
            high = square.astype(BF)
            low = (square - high.astype(F32)).astype(BF)
            line = (dot_nt(ones, high) + dot_nt(ones, low))[0:1]
            st[m, pl.ds(s * 8 + b, 1), :] = line
            if b == 7:
                rt[pl.ds(s, 1), :] = line
        return c

    lax.fori_loop(0, SEQS, sums, 0)
    pl.semaphore_wait(barrier, (NM - 1) + (NC - 1) + 9 + 2 * (NM - 1))

    def send_stat(t, c):
        remote(st.at[m], st.at[m], st_send, st_recv, (me, (m + t) % NM)).start()
        return c

    lax.fori_loop(1, NM, send_stat, 0)

    def send_rim(t, c):
        remote(rt, rr.at[m], rt_send, rt_recv, (after, (m + t) % NM)).start()
        return c

    lax.fori_loop(0, NM, send_rim, 0)
    remote(x_ref.at[:, pl.ds(TOK - 16, 16), :], rimx, rx_send, rx_recv, (after, m)).start()
    for n, piece in enumerate((up_piece, down_piece, out_piece)):
        here = piece(m, shard)
        remote(here, here, wa_send.at[n], wa_recv.at[n], (me, mate)).start()

    def spread(block):
        def send(t, c):
            for n, piece in enumerate((up_piece, down_piece, out_piece)):
                here = piece(block, shard)
                remote(here, here, wb_send.at[n], wb_recv.at[n], plane_peer(t)).start()
            return c

        lax.fori_loop(1, 16, send, 0)

    spread(m)

    def send_stream(s):
        def send(t, c):
            to = (m + t) % NM
            remote(
                x_ref.at[s, pl.ds(mul(to * TS, TS), TS), :],
                x_s.at[s, :, pl.ds(mul(m * CH, CH), CH)],
                x_send.at[s],
                x_recv.at[s],
                (me, to),
            ).start()
            return c

        lax.fori_loop(1, NM, send, 0)

    for s in range(SEQS):
        send_stream(s)
    x_s[:, :, pl.ds(mul(m * CH, CH), CH)] = x_ref[:, pl.ds(mul(m * TS, TS), TS), :]

    eye_r = lax.broadcasted_iota(jnp.int32, (256, 256), 0)
    eye_c = lax.broadcasted_iota(jnp.int32, (256, 256), 1)
    turned = dot_nt(jnp.where(eye_r == eye_c, 1.0, 0.0).astype(BF), ii_ref[...]).astype(BF)

    def build(b, c):
        rows = pl.ds(mul(b * 256, 256), 256)
        ri = b * 256 + lax.broadcasted_iota(jnp.int32, (256, 256), 0)
        ci = lax.broadcasted_iota(jnp.int32, (256, 256), 1)
        one = jnp.where(ci == (ri >> 4) * 4 + (ri & 3), 1.0, 0.0).astype(BF)
        part = dot_nt(one, fi_ref[...])
        for a in range(4):
            w1[rows, a * 256 : (a + 1) * 256] = jnp.where(((ri >> 2) & 3) == a, part, 0.0).astype(BF)
        quarter = jnp.where(ci == (ri >> 2), 1.0, 0.0).astype(BF)
        lane = lax.broadcasted_iota(jnp.int32, (256, 4), 1)
        row = b * 256 + lax.broadcasted_iota(jnp.int32, (256, 4), 0)
        for hot, factor, which, to in (
            (one, tw_ref, (row >> 2) & 3, twb),
            (quarter, bt_ref, row & 3, btb),
        ):
            part = lax.dot_general(
                hot.astype(F32),
                factor[...],
                (((1,), (1,)), ((), ())),
                precision=lax.Precision.HIGHEST,
                preferred_element_type=F32,
            )
            line = jnp.sum(jnp.where(lane == which, part, 0.0), axis=1, keepdims=True)
            to[rows, :] = jnp.broadcast_to(line, (256, 128))
        rq = lax.broadcasted_iota(jnp.int32, (256, 1024), 0)
        cq = lax.broadcasted_iota(jnp.int32, (256, 1024), 1)
        widen = jnp.where(rq == (cq >> 2), 1.0, 0.0).astype(BF)
        keep = (rq & 3) == (cq & 3)
        for factor, w in ((fo_ref, w2), (io_ref, w3)):
            part = dot_nt(quarter, factor[...]).astype(BF)
            w[rows, :] = jnp.where(keep, dot(part, widen), 0.0).astype(BF)
        pick = jnp.where(rq == (cq >> 4) * 4 + (cq & 3), 1.0, 0.0).astype(BF)
        w4[rows, :] = jnp.where(((cq >> 2) & 3) == b, dot(turned, pick), 0.0).astype(BF)
        return c

    lax.fori_loop(0, 4, build, 0)

    remote(st.at[pl.ds(0, 7)], st.at[pl.ds(0, 7)], st_send, st_recv, (me, mate)).wait_recv()
    total = st[0]
    for b in range(1, NM):
        total = total + st[b]
    scr[0:STAT_ROWS, :] = lax.rsqrt(total / D + EPS)
    for b in range(NM):
        gain2[:, b * CH : (b + 1) * CH] = st[b, 32:33, :]
    gain = gain_ref[0:1, :]

    def column(row):
        line = scr[pl.ds(row, 1), :]
        return jnp.transpose(jnp.broadcast_to(line, (128, 128)))

    remote(rr, rr, rt_send, rt_recv, (me, mate)).wait_recv()
    remote(rimx, rimx, rx_send, rx_recv, (me, mate)).wait_recv()
    total = rr[0]
    for b in range(1, NM):
        total = total + rr[b]
    scr[STAT_ROWS : STAT_ROWS + 8, :] = lax.rsqrt(total / D + EPS)
    for s in range(SEQS):
        rows = rimx[s].astype(F32)[8:16] * column(STAT_ROWS + s)[120:128] * gain
        edge = dot(jnp.concatenate([rows, rows], 0).astype(BF), projin_ref[...])[:8]
        edge = edge.astype(BF).astype(F32)
        rimp[s * 8 : s * 8 + 8, :] = jnp.where(me > 0, edge, 0.0)

    def ctx_copy(t, base, out_buf, in_buf, send, recv):
        to = (me + t) % NC
        return remote(
            out_buf.at[pl.ds(mul(base + to * 16, 16), 16), :],
            in_buf.at[pl.ds(mul(base + me * 16, 16), 16), :],
            send,
            recv,
            (to, m),
        )

    def whole_ctx(base, buf, send, recv):
        view = buf.at[pl.ds(mul(base, 16), 1008), :]
        return remote(view, view, send, recv, (me, mate))

    def send_first(s):
        def send(t, c):
            ctx_copy(t, s * TOK, s1, r1, c1_send.at[s], c1_recv.at[s]).start()
            return c

        lax.fori_loop(1, NC, send, 0)

    def forward(s, c):
        base = s * TOK

        def project(b, c2):
            rows = x_ref[s, pl.ds(mul(b * 128, 128), 128), :].astype(F32)
            normed = (rows * column(s * 8 + b) * gain).astype(BF)
            pj[pl.ds(mul(8 + b * 128, 8), 128), :] = (
                dot(normed, projin_ref[...]).astype(BF).astype(F32)
            )
            return c2

        pj[0:8, :] = rimp[pl.ds(mul(s * 8, 8), 8), :]
        lax.fori_loop(0, 8, project, 0)
        for b in range(8):
            lo = b * 128
            mixed = (
                taps_ref[0] * pj[8 + lo : 136 + lo, :]
                + taps_ref[1] * pj[7 + lo : 135 + lo, :]
                + taps_ref[2] * pj[6 + lo : 134 + lo, :]
            )
            q_s[pl.ds(mul(base + lo, 128), 128), :] = mixed[:, :CH].astype(BF)
            src[lo : lo + 128, :] = (mixed[:, CH : 2 * CH] * mixed[:, 2 * CH :]).astype(BF)

        def inner(b, c2):
            rows = pl.ds(mul(b * 256, 256), 256)
            first = dot(w1[rows, :], src[...]) * twb[rows, :]
            s1[pl.ds(mul(base + b * 256, 256), 256), :] = first.astype(BF)
            return c2

        lax.fori_loop(0, 4, inner, 0)

        send_first(s)

        own = pl.ds(mul(base + me * 16, 16), 16)
        r1[own, :] = s1[own, :]

        @pl.when(s == 0)
        def _():
            for n, piece in enumerate((up_piece, down_piece, out_piece)):
                there = piece(mate, shard)
                remote(there, there, wa_send.at[n], wa_recv.at[n], (me, mate)).wait_recv()
            spread(mate)

        return c

    lax.fori_loop(0, SEQS, forward, 0)

    up_all = r1.at[pl.ds(0, 30 * 64), :]
    out_all = r1.at[pl.ds(0, 30 * 16), :]
    for n, view in enumerate((up_all, up_all, out_all)):
        remote(view, view, wb_send.at[n], wb_recv.at[n], (me, mate)).wait_recv()

    def halves(side):
        return (
            upw.at[:, pl.ds(mul(side * 64, 64), 64), :],
            dx.at[:, pl.ds(mul(side * 512, 512), 512), :],
            pw.at[pl.ds(mul(side * 512, 512), 512), :],
        )

    for n, half in enumerate(halves(core)):
        remote(half, half, ws_send.at[n], ws_recv.at[n], (twin, m)).start()

    def middle(s, c):
        base = s * TOK
        whole_ctx(base, r1, c1_send.at[s], c1_recv.at[s]).wait_recv()


        def outer(b, c2):
            rows = pl.ds(mul(b * 256, 256), 256)
            got = r1[pl.ds(mul(base, 1024), 1024), :]
            sec[rows, :] = (dot(w2[rows, :], got) * kern_ref[rows, :].astype(F32)).astype(BF)
            return c2

        lax.fori_loop(0, 4, outer, 0)

        def back(b, c2):
            rows = pl.ds(mul(b * 256, 256), 256)
            third = dot(w3[rows, :], sec[...]) * btb[rows, :]
            s2[pl.ds(mul(base + b * 256, 256), 256), :] = third.astype(BF)
            return c2

        lax.fori_loop(0, 4, back, 0)

        def send(t, c2):
            ctx_copy(t, base, s2, r2, c2_send.at[s], c2_recv.at[s]).start()
            return c2

        lax.fori_loop(1, NC, send, 0)
        own = pl.ds(mul(base + me * 16, 16), 16)
        r2[own, :] = s2[own, :]
        return c

    lax.fori_loop(0, SEQS, middle, 0)

    def gate_in(s, c):
        whole_ctx(s * TOK, r2, c2_send.at[s], c2_recv.at[s]).wait_recv()
        return c

    lax.fori_loop(0, SEQS, gate_in, 0)

    def gate(s, c):
        base = s * TOK

        def last(b, c2):
            rows = pl.ds(mul(b * 256, 256), 256)
            here = pl.ds(mul(base + b * 256, 256), 256)
            conv = dot(w4[rows, :], r2[pl.ds(mul(base, 1024), 1024), :])
            gt[here, :] = (q_s[here, :].astype(F32) * conv).astype(BF)
            return c2

        lax.fori_loop(0, 4, last, 0)

        def send(t, c2):
            to = (m + t) % NM
            remote(
                gt.at[pl.ds(mul(base + to * TS, TS), TS), :],
                g_s.at[s, :, pl.ds(mul(m * CH, CH), CH)],
                g_send.at[s],
                g_recv.at[s],
                (me, to),
            ).start()
            return c2

        lax.fori_loop(1, NM, send, 0)
        g_s[s, :, pl.ds(mul(m * CH, CH), CH)] = gt[pl.ds(mul(base + m * TS, TS), TS), :]
        return c

    lax.fori_loop(0, SEQS, gate, 0)

    for n, half in enumerate(halves(1 - core)):
        remote(half, half, ws_send.at[n], ws_recv.at[n], (twin, m)).wait_recv()

    def finish(s, c):
        g_all = g_s.at[s, :, pl.ds(0, 7 * CH)]
        remote(g_all, g_all, g_send.at[s], g_recv.at[s], (me, mate)).wait_recv()
        remote(g_all, g_all, x_send.at[s], x_recv.at[s], (me, mate)).wait_recv()
        resid = (x_s[s].astype(F32) + dot(g_s[s], pw[...])).astype(BF).astype(F32)
        sumsq = jnp.sum(resid * resid, axis=1, keepdims=True)
        normed = (resid * lax.rsqrt(sumsq / D + EPS) * gain2[...]).astype(BF)
        for i in range(NM):
            act = jax.nn.gelu(dot(normed[:, i * CH : (i + 1) * CH], upw[i])).astype(BF)
            for jj in range(4):
                h_s[jj, :, i * 128 : (i + 1) * 128] = act[:, jj * 128 : (jj + 1) * 128]
        for jj in range(4):
            low = dot(h_s[jj], dx[jj]) + resid[:, jj * 256 : (jj + 1) * 256]
            ob[s, 2 * jj] = low[:, :CH].astype(BF)
            ob[s, 2 * jj + 1] = low[:, CH:].astype(BF)

        rows = pl.ds(mul(s * TOK + m * TS, TS), TS)

        def send(t, c2):
            to = (m + t) % NM
            remote(ob.at[s, to], os_.at[rows, :], o_send, o_recv, (me, to)).start()
            return c2

        lax.fori_loop(1, NM, send, 0)
        os_[rows, :] = ob[s, m]
        return c

    lax.fori_loop(0, SEQS, finish, 0)

    o_all = os_.at[pl.ds(0, 28 * TS), :]
    remote(o_all, o_all, o_send, o_recv, (me, mate)).wait()
    remote(st.at[pl.ds(0, 7)], st.at[pl.ds(0, 7)], st_send, st_recv, (me, mate)).wait_send()
    for n, piece in enumerate((up_piece, down_piece, out_piece)):
        here = piece(m, shard)
        remote(here, here, wa_send.at[n], wa_recv.at[n], (me, mate)).wait_send()
    for n, view in enumerate((up_all, up_all, out_all)):
        remote(view, view, wb_send.at[n], wb_recv.at[n], (me, mate)).wait_send()
    for n, half in enumerate(halves(core)):
        remote(half, half, ws_send.at[n], ws_recv.at[n], (twin, m)).wait_send()
    remote(rr, rr, rt_send, rt_recv, (me, mate)).wait_send()
    remote(rimx, rimx, rx_send, rx_recv, (me, mate)).wait_send()

    def drain(s, c):
        base = s * TOK
        whole_ctx(base, s1, c1_send.at[s], c1_recv.at[s]).wait_send()
        whole_ctx(base, s2, c2_send.at[s], c2_recv.at[s]).wait_send()
        g_all = g_s.at[s, :, pl.ds(0, 7 * CH)]
        remote(g_all, g_all, g_send.at[s], g_recv.at[s], (me, mate)).wait_send()
        remote(g_all, g_all, x_send.at[s], x_recv.at[s], (me, mate)).wait_send()
        return c

    lax.fori_loop(0, SEQS, drain, 0)
    out_ref[...] = os_[...]


def body(
    stream,
    gain_mix,
    proj_in,
    short_taps,
    fwd_inner,
    twid_inner,
    fwd_outer,
    kernel_grid,
    inv_outer,
    backward_twiddle,
    inv_inner,
    proj_out,
    gain_mlp,
    up_blocks,
    down_blocks,
):
    gains = jnp.stack([gain_mix, gain_mlp]).astype(F32)
    operands = (
        stream,
        gains,
        proj_in[0],
        short_taps,
        fwd_inner,
        twid_inner,
        fwd_outer,
        kernel_grid.reshape(TOK, CH),
        inv_outer,
        backward_twiddle.T,
        inv_inner,
        proj_out[0],
        up_blocks[0],
        down_blocks[0],
    )
    vmem = pl.BlockSpec(memory_space=pltpu.VMEM)
    dma = pltpu.SemaphoreType.DMA
    flat = pltpu.VMEM((SEQS * TOK, CH), BF)
    square = pltpu.VMEM((1024, 1024), BF)
    out = pl.pallas_call(
        kernel,
        out_shape=jax.ShapeDtypeStruct((SEQS * TOK, CH), BF),
        in_specs=[vmem] * len(operands),
        out_specs=vmem,
        scratch_shapes=[
            square,
            square,
            square,
            square,
            square,
            pltpu.VMEM((NM, CH, 512), BF),
            pltpu.VMEM((4, 1024, 256), BF),
            pltpu.VMEM((NM, STAT_ROWS, 128), F32),
            pltpu.VMEM((8, 128), F32),
            pltpu.VMEM((NM, 8, 128), F32),
            pltpu.VMEM((SEQS, 16, CH), BF),
            pltpu.VMEM((TOK, 128), F32),
            pltpu.VMEM((TOK, 128), F32),
            pltpu.VMEM((STAT_ROWS + 8, 128), F32),
            pltpu.VMEM((1, 1024), F32),
            pltpu.VMEM((32, 3 * CH), F32),
            pltpu.VMEM((8 + TOK, 3 * CH), F32),
            pltpu.VMEM((TOK, CH), BF),
            flat,
            flat,
            flat,
            pltpu.VMEM((TOK, CH), BF),
            flat,
            flat,
            flat,
            pltpu.VMEM((SEQS, TS, 1024), BF),
            pltpu.VMEM((SEQS, TS, 1024), BF),
            pltpu.VMEM((4, TS, 1024), BF),
            pltpu.VMEM((SEQS, NM, TS, CH), BF),
            flat,
            dma,
            dma,
            dma((SEQS,)),
            dma((SEQS,)),
            dma((3,)),
            dma((3,)),
            dma((3,)),
            dma((3,)),
            dma((3,)),
            dma((3,)),
            dma,
            dma,
            dma,
            dma,
            dma((SEQS,)),
            dma((SEQS,)),
            dma((SEQS,)),
            dma((SEQS,)),
            dma((SEQS,)),
            dma((SEQS,)),
            dma,
            dma,
        ],
        compiler_params=pltpu.CompilerParams(
            collective_id=0, has_side_effects=True, vmem_limit_bytes=60 * 1024 * 1024
        ),
        name="monarch_block",
    )(*operands)
    return out.reshape(SEQS, TOK, CH)


def solution(mesh):
    placed = (
        P(None, "ctx", "mp"),
        P("mp"),
        P("mp", None, None),
        P(None, "mp", None),
        P(),
        P("ctx", None),
        P(),
        P(None, "ctx", "mp"),
        P(),
        P(None, "ctx"),
        P(),
        P("mp", None, None),
        P("mp"),
        P("mp", None, None),
        P("mp", None, None),
    )
    return jax.shard_map(
        body, mesh=mesh, in_specs=placed, out_specs=P(None, "ctx", "mp"), check_vma=False
    )
```

```python
import functools

import jax
import jax.numpy as jnp
from jax import lax
from jax.experimental import pallas as pl
from jax.experimental.pallas import tpu as pltpu
from jax.sharding import PartitionSpec as P

D = 1024
EPS = 1e-05
BF = jnp.bfloat16
F32 = jnp.float32
MESH = pl.DeviceIdType.MESH

SEQS = 4
TOK = 1024
CH = 128
NC = 64
NM = 8
TS = TOK // NM
STAT_ROWS = 40


def dot(a, b):
    return jnp.dot(a, b, preferred_element_type=F32)


def dot_nt(a, b):
    return lax.dot_general(a, b, (((1,), (1,)), ((), ())), preferred_element_type=F32)


def mul(v, n):
    return pl.multiple_of(v, n)


def kernel(
    x_ref,
    gain_ref,
    projin_ref,
    taps_ref,
    fi_ref,
    tw_ref,
    fo_ref,
    kern_ref,
    io_ref,
    bt_ref,
    ii_ref,
    projout_ref,
    up_ref,
    down_ref,
    out_ref,
    w1,
    w2,
    w3,
    w4,
    pw,
    upw,
    dx,
    st,
    rt,
    rr,
    rimx,
    twb,
    btb,
    scr,
    gain2,
    rimp,
    pj,
    src,
    q_s,
    s1,
    r1,
    sec,
    s2,
    r2,
    gt,
    g_s,
    x_s,
    h_s,
    ob,
    os_,
    st_send,
    st_recv,
    x_send,
    x_recv,
    wa_send,
    wa_recv,
    wb_send,
    wb_recv,
    ws_send,
    ws_recv,
    rt_send,
    rt_recv,
    rx_send,
    rx_recv,
    c1_send,
    c1_recv,
    c2_send,
    c2_recv,
    g_send,
    g_recv,
    o_send,
    o_recv,
):
    me = lax.axis_index("ctx")
    m = lax.axis_index("mp")
    core = me % 2
    y_pos = me // 16
    z_lo = (me // 2) % 8
    shard = core * 4 + y_pos
    x_pos = m // 2
    z_hi = m % 2
    mate = x_pos * 2 + (1 - z_hi)
    twin = me + 1 - 2 * core
    after = (me + 1) % NC
    before = (me + NC - 1) % NC

    def plane_peer(t):
        x_to = (x_pos + t // 4) % 4
        y_to = (y_pos + t % 4) % 4
        return y_to * 16 + z_lo * 2 + core, x_to * 2 + z_hi

    def remote(src_view, dst_view, send, recv, to):
        return pltpu.make_async_remote_copy(
            src_ref=src_view,
            dst_ref=dst_view,
            send_sem=send,
            recv_sem=recv,
            device_id=to,
            device_id_type=MESH,
        )

    def up_piece(b, s):
        return upw.at[b, pl.ds(mul(s * 16, 16), 16), :]

    def down_piece(b, s):
        return dx.at[
            b // 2,
            pl.ds(mul(s * 128 + (b % 2) * 64, 64), 64),
            pl.ds(mul((b % 2) * 128, 128), 128),
        ]

    def out_piece(b, s):
        return pw.at[pl.ds(mul(s * 128 + b * 16, 16), 16), pl.ds(mul(b * 128, 128), 128)]

    def clear_pw(i, c):
        pw[pl.ds(mul(i * 128, 128), 128), :] = jnp.zeros((128, 1024), BF)
        return c

    lax.fori_loop(0, 8, clear_pw, 0)

    def clear_dx(i, c):
        dx[i] = jnp.zeros((1024, 256), BF)
        return c

    lax.fori_loop(0, 4, clear_dx, 0)
    barrier = pltpu.get_barrier_semaphore()

    def greet_mp(t, c):
        pl.semaphore_signal(barrier, inc=1, device_id=(me, (m + t) % NM), device_id_type=MESH)
        return c

    lax.fori_loop(1, NM, greet_mp, 0)

    def greet_ctx(t, c):
        pl.semaphore_signal(barrier, inc=1, device_id=((me + t) % NC, m), device_id_type=MESH)
        return c

    lax.fori_loop(1, NC, greet_ctx, 0)

    def greet_plane(t, c):
        to = plane_peer(4 * (1 + t // 3) + 1 + t % 3)
        pl.semaphore_signal(barrier, inc=1, device_id=to, device_id_type=MESH)
        return c

    lax.fori_loop(0, 9, greet_plane, 0)

    def greet_rim(t, c):
        to = (m + t) % NM
        pl.semaphore_signal(barrier, inc=1, device_id=(after, to), device_id_type=MESH)
        pl.semaphore_signal(barrier, inc=1, device_id=(before, to), device_id_type=MESH)
        return c

    lax.fori_loop(1, NM, greet_rim, 0)

    up_piece(m, shard)[...] = up_ref[pl.ds(mul(shard * 16, 16), 16), :]
    down_piece(m, shard)[...] = down_ref[pl.ds(mul(shard * 64, 64), 64), :]
    out_piece(m, shard)[...] = projout_ref[pl.ds(mul(shard * 16, 16), 16), :]
    ones = jnp.ones((8, CH), BF)
    rt[...] = jnp.zeros((8, 128), F32)
    st[m, 32:40, :] = jnp.broadcast_to(gain_ref[1:2, :], (8, 128))

    def sums(s, c):
        for b in range(8):
            rows = x_ref[s, b * 128 : (b + 1) * 128, :].astype(F32)
            square = rows * rows
            high = square.astype(BF)
            low = (square - high.astype(F32)).astype(BF)
            line = (dot_nt(ones, high) + dot_nt(ones, low))[0:1]
            st[m, pl.ds(s * 8 + b, 1), :] = line
            if b == 7:
                rt[pl.ds(s, 1), :] = line
        return c

    lax.fori_loop(0, SEQS, sums, 0)
    pl.semaphore_wait(barrier, (NM - 1) + (NC - 1) + 9 + 2 * (NM - 1))

    def send_stat(t, c):
        remote(st.at[m], st.at[m], st_send, st_recv, (me, (m + t) % NM)).start()
        return c

    lax.fori_loop(1, NM, send_stat, 0)

    def send_rim(t, c):
        remote(rt, rr.at[m], rt_send, rt_recv, (after, (m + t) % NM)).start()
        return c

    lax.fori_loop(0, NM, send_rim, 0)
    remote(x_ref.at[:, pl.ds(TOK - 16, 16), :], rimx, rx_send, rx_recv, (after, m)).start()
    for n, piece in enumerate((up_piece, down_piece, out_piece)):
        here = piece(m, shard)
        remote(here, here, wa_send.at[n], wa_recv.at[n], (me, mate)).start()

    def spread(block):
        def send(t, c):
            for n, piece in enumerate((up_piece, down_piece, out_piece)):
                here = piece(block, shard)
                remote(here, here, wb_send.at[n], wb_recv.at[n], plane_peer(t)).start()
            return c

        lax.fori_loop(1, 16, send, 0)

    spread(m)

    def send_stream(s):
        def send(t, c):
            to = (m + t) % NM
            remote(
                x_ref.at[s, pl.ds(mul(to * TS, TS), TS), :],
                x_s.at[s, :, pl.ds(mul(m * CH, CH), CH)],
                x_send.at[s],
                x_recv.at[s],
                (me, to),
            ).start()
            return c

        lax.fori_loop(1, NM, send, 0)

    for s in range(SEQS):
        send_stream(s)
    x_s[:, :, pl.ds(mul(m * CH, CH), CH)] = x_ref[:, pl.ds(mul(m * TS, TS), TS), :]

    eye_r = lax.broadcasted_iota(jnp.int32, (256, 256), 0)
    eye_c = lax.broadcasted_iota(jnp.int32, (256, 256), 1)
    turned = dot_nt(jnp.where(eye_r == eye_c, 1.0, 0.0).astype(BF), ii_ref[...]).astype(BF)

    def build(b, c):
        rows = pl.ds(mul(b * 256, 256), 256)
        ri = b * 256 + lax.broadcasted_iota(jnp.int32, (256, 256), 0)
        ci = lax.broadcasted_iota(jnp.int32, (256, 256), 1)
        one = jnp.where(ci == (ri >> 4) * 4 + (ri & 3), 1.0, 0.0).astype(BF)
        part = dot_nt(one, fi_ref[...])
        for a in range(4):
            w1[rows, a * 256 : (a + 1) * 256] = jnp.where(((ri >> 2) & 3) == a, part, 0.0).astype(BF)
        quarter = jnp.where(ci == (ri >> 2), 1.0, 0.0).astype(BF)
        lane = lax.broadcasted_iota(jnp.int32, (256, 4), 1)
        row = b * 256 + lax.broadcasted_iota(jnp.int32, (256, 4), 0)
        for hot, factor, which, to in (
            (one, tw_ref, (row >> 2) & 3, twb),
            (quarter, bt_ref, row & 3, btb),
        ):
            part = lax.dot_general(
                hot.astype(F32),
                factor[...],
                (((1,), (1,)), ((), ())),
                precision=lax.Precision.HIGHEST,
                preferred_element_type=F32,
            )
            line = jnp.sum(jnp.where(lane == which, part, 0.0), axis=1, keepdims=True)
            to[rows, :] = jnp.broadcast_to(line, (256, 128))
        rq = lax.broadcasted_iota(jnp.int32, (256, 1024), 0)
        cq = lax.broadcasted_iota(jnp.int32, (256, 1024), 1)
        widen = jnp.where(rq == (cq >> 2), 1.0, 0.0).astype(BF)
        keep = (rq & 3) == (cq & 3)
        for factor, w in ((fo_ref, w2), (io_ref, w3)):
            part = dot_nt(quarter, factor[...]).astype(BF)
            w[rows, :] = jnp.where(keep, dot(part, widen), 0.0).astype(BF)
        pick = jnp.where(rq == (cq >> 4) * 4 + (cq & 3), 1.0, 0.0).astype(BF)
        w4[rows, :] = jnp.where(((cq >> 2) & 3) == b, dot(turned, pick), 0.0).astype(BF)
        return c

    lax.fori_loop(0, 4, build, 0)

    remote(st.at[pl.ds(0, 7)], st.at[pl.ds(0, 7)], st_send, st_recv, (me, mate)).wait_recv()
    total = st[0]
    for b in range(1, NM):
        total = total + st[b]
    scr[0:STAT_ROWS, :] = lax.rsqrt(total / D + EPS)
    for b in range(NM):
        gain2[:, b * CH : (b + 1) * CH] = st[b, 32:33, :]
    gain = gain_ref[0:1, :]

    def column(row):
        line = scr[pl.ds(row, 1), :]
        return jnp.transpose(jnp.broadcast_to(line, (128, 128)))

    remote(rr, rr, rt_send, rt_recv, (me, mate)).wait_recv()
    remote(rimx, rimx, rx_send, rx_recv, (me, mate)).wait_recv()
    total = rr[0]
    for b in range(1, NM):
        total = total + rr[b]
    scr[STAT_ROWS : STAT_ROWS + 8, :] = lax.rsqrt(total / D + EPS)
    for s in range(SEQS):
        rows = rimx[s].astype(F32)[8:16] * column(STAT_ROWS + s)[120:128] * gain
        edge = dot(jnp.concatenate([rows, rows], 0).astype(BF), projin_ref[...])[:8]
        edge = edge.astype(BF).astype(F32)
        rimp[s * 8 : s * 8 + 8, :] = jnp.where(me > 0, edge, 0.0)

    def ctx_copy(t, base, out_buf, in_buf, send, recv):
        to = (me + t) % NC
        return remote(
            out_buf.at[pl.ds(mul(base + to * 16, 16), 16), :],
            in_buf.at[pl.ds(mul(base + me * 16, 16), 16), :],
            send,
            recv,
            (to, m),
        )

    def whole_ctx(base, buf, send, recv):
        view = buf.at[pl.ds(mul(base, 16), 1008), :]
        return remote(view, view, send, recv, (me, mate))

    def send_first(s):
        def send(t, c):
            ctx_copy(t, s * TOK, s1, r1, c1_send.at[s], c1_recv.at[s]).start()
            return c

        lax.fori_loop(1, NC, send, 0)

    def forward(s, c):
        base = s * TOK

        def project(b, c2):
            rows = x_ref[s, pl.ds(mul(b * 128, 128), 128), :].astype(F32)
            normed = (rows * column(s * 8 + b) * gain).astype(BF)
            pj[pl.ds(mul(8 + b * 128, 8), 128), :] = (
                dot(normed, projin_ref[...]).astype(BF).astype(F32)
            )
            return c2

        pj[0:8, :] = rimp[pl.ds(mul(s * 8, 8), 8), :]
        lax.fori_loop(0, 8, project, 0)
        for b in range(8):
            lo = b * 128
            mixed = (
                taps_ref[0] * pj[8 + lo : 136 + lo, :]
                + taps_ref[1] * pj[7 + lo : 135 + lo, :]
                + taps_ref[2] * pj[6 + lo : 134 + lo, :]
            )
            q_s[pl.ds(mul(base + lo, 128), 128), :] = mixed[:, :CH].astype(BF)
            src[lo : lo + 128, :] = (mixed[:, CH : 2 * CH] * mixed[:, 2 * CH :]).astype(BF)

        def inner(b, c2):
            rows = pl.ds(mul(b * 256, 256), 256)
            first = dot(w1[rows, :], src[...]) * twb[rows, :]
            s1[pl.ds(mul(base + b * 256, 256), 256), :] = first.astype(BF)
            return c2

        lax.fori_loop(0, 4, inner, 0)

        send_first(s)

        own = pl.ds(mul(base + me * 16, 16), 16)
        r1[own, :] = s1[own, :]

        @pl.when(s == 0)
        def _():
            for n, piece in enumerate((up_piece, down_piece, out_piece)):
                there = piece(mate, shard)
                remote(there, there, wa_send.at[n], wa_recv.at[n], (me, mate)).wait_recv()
            spread(mate)

        return c

    lax.fori_loop(0, SEQS, forward, 0)

    up_all = r1.at[pl.ds(0, 30 * 64), :]
    out_all = r1.at[pl.ds(0, 30 * 16), :]
    for n, view in enumerate((up_all, up_all, out_all)):
        remote(view, view, wb_send.at[n], wb_recv.at[n], (me, mate)).wait_recv()

    def halves(side):
        return (
            upw.at[:, pl.ds(mul(side * 64, 64), 64), :],
            dx.at[:, pl.ds(mul(side * 512, 512), 512), :],
            pw.at[pl.ds(mul(side * 512, 512), 512), :],
        )

    for n, half in enumerate(halves(core)):
        remote(half, half, ws_send.at[n], ws_recv.at[n], (twin, m)).start()

    def middle(s, c):
        base = s * TOK
        whole_ctx(base, r1, c1_send.at[s], c1_recv.at[s]).wait_recv()


        def outer(b, c2):
            rows = pl.ds(mul(b * 256, 256), 256)
            got = r1[pl.ds(mul(base, 1024), 1024), :]
            sec[rows, :] = (dot(w2[rows, :], got) * kern_ref[rows, :].astype(F32)).astype(BF)
            return c2

        lax.fori_loop(0, 4, outer, 0)

        def back(b, c2):
            rows = pl.ds(mul(b * 256, 256), 256)
            third = dot(w3[rows, :], sec[...]) * btb[rows, :]
            s2[pl.ds(mul(base + b * 256, 256), 256), :] = third.astype(BF)
            return c2

        lax.fori_loop(0, 4, back, 0)

        def send(t, c2):
            ctx_copy(t, base, s2, r2, c2_send.at[s], c2_recv.at[s]).start()
            return c2

        lax.fori_loop(1, NC, send, 0)
        own = pl.ds(mul(base + me * 16, 16), 16)
        r2[own, :] = s2[own, :]
        return c

    lax.fori_loop(0, SEQS, middle, 0)

    def gate(s, c):
        base = s * TOK
        whole_ctx(base, r2, c2_send.at[s], c2_recv.at[s]).wait_recv()

        def last(b, c2):
            rows = pl.ds(mul(b * 256, 256), 256)
            here = pl.ds(mul(base + b * 256, 256), 256)
            conv = dot(w4[rows, :], r2[pl.ds(mul(base, 1024), 1024), :])
            gt[here, :] = (q_s[here, :].astype(F32) * conv).astype(BF)
            return c2

        lax.fori_loop(0, 4, last, 0)
        return c

    lax.fori_loop(0, SEQS, gate, 0)

    def gated_out(s, c):
        base = s * TOK

        def send(t, c2):
            to = (m + t) % NM
            remote(
                gt.at[pl.ds(mul(base + to * TS, TS), TS), :],
                g_s.at[s, :, pl.ds(mul(m * CH, CH), CH)],
                g_send.at[s],
                g_recv.at[s],
                (me, to),
            ).start()
            return c2

        lax.fori_loop(1, NM, send, 0)
        g_s[s, :, pl.ds(mul(m * CH, CH), CH)] = gt[pl.ds(mul(base + m * TS, TS), TS), :]
        return c

    lax.fori_loop(0, SEQS, gated_out, 0)

    for n, half in enumerate(halves(1 - core)):
        remote(half, half, ws_send.at[n], ws_recv.at[n], (twin, m)).wait_recv()

    def finish(s, c):
        g_all = g_s.at[s, :, pl.ds(0, 7 * CH)]
        remote(g_all, g_all, g_send.at[s], g_recv.at[s], (me, mate)).wait_recv()
        remote(g_all, g_all, x_send.at[s], x_recv.at[s], (me, mate)).wait_recv()
        resid = (x_s[s].astype(F32) + dot(g_s[s], pw[...])).astype(BF).astype(F32)
        sumsq = jnp.sum(resid * resid, axis=1, keepdims=True)
        normed = (resid * lax.rsqrt(sumsq / D + EPS) * gain2[...]).astype(BF)
        for i in range(NM):
            act = jax.nn.gelu(dot(normed[:, i * CH : (i + 1) * CH], upw[i])).astype(BF)
            for jj in range(4):
                h_s[jj, :, i * 128 : (i + 1) * 128] = act[:, jj * 128 : (jj + 1) * 128]
        for jj in range(4):
            low = dot(h_s[jj], dx[jj]) + resid[:, jj * 256 : (jj + 1) * 256]
            ob[s, 2 * jj] = low[:, :CH].astype(BF)
            ob[s, 2 * jj + 1] = low[:, CH:].astype(BF)

        rows = pl.ds(mul(s * TOK + m * TS, TS), TS)

        def send(t, c2):
            to = (m + t) % NM
            remote(ob.at[s, to], os_.at[rows, :], o_send, o_recv, (me, to)).start()
            return c2

        lax.fori_loop(1, NM, send, 0)
        os_[rows, :] = ob[s, m]
        return c

    lax.fori_loop(0, SEQS, finish, 0)

    o_all = os_.at[pl.ds(0, 28 * TS), :]
    remote(o_all, o_all, o_send, o_recv, (me, mate)).wait()
    remote(st.at[pl.ds(0, 7)], st.at[pl.ds(0, 7)], st_send, st_recv, (me, mate)).wait_send()
    for n, piece in enumerate((up_piece, down_piece, out_piece)):
        here = piece(m, shard)
        remote(here, here, wa_send.at[n], wa_recv.at[n], (me, mate)).wait_send()
    for n, view in enumerate((up_all, up_all, out_all)):
        remote(view, view, wb_send.at[n], wb_recv.at[n], (me, mate)).wait_send()
    for n, half in enumerate(halves(core)):
        remote(half, half, ws_send.at[n], ws_recv.at[n], (twin, m)).wait_send()
    remote(rr, rr, rt_send, rt_recv, (me, mate)).wait_send()
    remote(rimx, rimx, rx_send, rx_recv, (me, mate)).wait_send()

    def drain(s, c):
        base = s * TOK
        whole_ctx(base, s1, c1_send.at[s], c1_recv.at[s]).wait_send()
        whole_ctx(base, s2, c2_send.at[s], c2_recv.at[s]).wait_send()
        g_all = g_s.at[s, :, pl.ds(0, 7 * CH)]
        remote(g_all, g_all, g_send.at[s], g_recv.at[s], (me, mate)).wait_send()
        remote(g_all, g_all, x_send.at[s], x_recv.at[s], (me, mate)).wait_send()
        return c

    lax.fori_loop(0, SEQS, drain, 0)
    out_ref[...] = os_[...]


def body(
    stream,
    gain_mix,
    proj_in,
    short_taps,
    fwd_inner,
    twid_inner,
    fwd_outer,
    kernel_grid,
    inv_outer,
    backward_twiddle,
    inv_inner,
    proj_out,
    gain_mlp,
    up_blocks,
    down_blocks,
):
    gains = jnp.stack([gain_mix, gain_mlp]).astype(F32)
    operands = (
        stream,
        gains,
        proj_in[0],
        short_taps,
        fwd_inner,
        twid_inner,
        fwd_outer,
        kernel_grid.reshape(TOK, CH),
        inv_outer,
        backward_twiddle.T,
        inv_inner,
        proj_out[0],
        up_blocks[0],
        down_blocks[0],
    )
    vmem = pl.BlockSpec(memory_space=pltpu.VMEM)
    dma = pltpu.SemaphoreType.DMA
    flat = pltpu.VMEM((SEQS * TOK, CH), BF)
    square = pltpu.VMEM((1024, 1024), BF)
    out = pl.pallas_call(
        kernel,
        out_shape=jax.ShapeDtypeStruct((SEQS * TOK, CH), BF),
        in_specs=[vmem] * len(operands),
        out_specs=vmem,
        scratch_shapes=[
            square,
            square,
            square,
            square,
            square,
            pltpu.VMEM((NM, CH, 512), BF),
            pltpu.VMEM((4, 1024, 256), BF),
            pltpu.VMEM((NM, STAT_ROWS, 128), F32),
            pltpu.VMEM((8, 128), F32),
            pltpu.VMEM((NM, 8, 128), F32),
            pltpu.VMEM((SEQS, 16, CH), BF),
            pltpu.VMEM((TOK, 128), F32),
            pltpu.VMEM((TOK, 128), F32),
            pltpu.VMEM((STAT_ROWS + 8, 128), F32),
            pltpu.VMEM((1, 1024), F32),
            pltpu.VMEM((32, 3 * CH), F32),
            pltpu.VMEM((8 + TOK, 3 * CH), F32),
            pltpu.VMEM((TOK, CH), BF),
            flat,
            flat,
            flat,
            pltpu.VMEM((TOK, CH), BF),
            flat,
            flat,
            flat,
            pltpu.VMEM((SEQS, TS, 1024), BF),
            pltpu.VMEM((SEQS, TS, 1024), BF),
            pltpu.VMEM((4, TS, 1024), BF),
            pltpu.VMEM((SEQS, NM, TS, CH), BF),
            flat,
            dma,
            dma,
            dma((SEQS,)),
            dma((SEQS,)),
            dma((3,)),
            dma((3,)),
            dma((3,)),
            dma((3,)),
            dma((3,)),
            dma((3,)),
            dma,
            dma,
            dma,
            dma,
            dma((SEQS,)),
            dma((SEQS,)),
            dma((SEQS,)),
            dma((SEQS,)),
            dma((SEQS,)),
            dma((SEQS,)),
            dma,
            dma,
        ],
        compiler_params=pltpu.CompilerParams(
            collective_id=0, has_side_effects=True, vmem_limit_bytes=60 * 1024 * 1024
        ),
        name="monarch_block",
    )(*operands)
    return out.reshape(SEQS, TOK, CH)


def solution(mesh):
    placed = (
        P(None, "ctx", "mp"),
        P("mp"),
        P("mp", None, None),
        P(None, "mp", None),
        P(),
        P("ctx", None),
        P(),
        P(None, "ctx", "mp"),
        P(),
        P(None, "ctx"),
        P(),
        P("mp", None, None),
        P("mp"),
        P("mp", None, None),
        P("mp", None, None),
    )
    return jax.shard_map(
        body, mesh=mesh, in_specs=placed, out_specs=P(None, "ctx", "mp"), check_vma=False
    )
```
